128 devices in a mesh: row: 8 (over z, core), col: 16 (over y, x).
Axes of the slice: x: 4, y: 4, z: 4, core: 2. Of those that a mesh axis runs over, the one named last changes fastest.
Arguments:
- wrf_forcing: float32 [7, 128, 256], P(None, ('row', 'col')), may hold values from 0 to 1
- ground_height_km: float32 [2048, 4096], P('row', 'col'), may hold values from 0.2 to 3
- reflected_share: float32 [2048, 4096], P('row', 'col'), may hold values from 0.35 to 0.85
- snow_water: float32 [2048, 4096], P('row', 'col'), may hold values from 0 to 6
- soil_water: float32 [2048, 4096], P('row', 'col'), may hold values from 1 to 8
- saturated: float32 [2048, 4096], P('row', 'col'), may hold values from 0.5 to 4
- release_rate: float32 [2048, 4096], P('row', 'col'), may hold values from 0.05 to 0.3
- mfd_weights: bfloat16 [8, 2048, 4096], P(None, 'row', 'col'), may hold values from 0 to 1, as said below
- cell_segment: int32 [2048, 4096], P('row', 'col'), may hold values from 0 to 127
- route_inverse: float32 [128, 2048, 128], P('row', 'col'), may hold values from 0 to 1, as said below
- transfer: float32 [128, 2048], P('row', 'col'), may hold values from 0.96 to 1
- downstream: int32 [128, 16], P('row', 'col'), may hold values from 1 to 16, as said below
Outputs:
- snowpack: float32 [2048, 4096], P('row', 'col')
- soil_moisture: float32 [2048, 4096], P('row', 'col')
- groundwater: float32 [2048, 4096], P('row', 'col')
- channel_flow: float32 [128, 2048], P('row', 'col')
The draws below stay inside these ranges and needn't reach their ends.
Inputs may be any that keep to these rules, and one draw needn't show every extreme that they name: `mfd_weights`: the eight shares of a cell are positive and add up to less than one. `route_inverse`: entries are positive and every column of each block's 128 by 128 matrix sums to one. `downstream`: block b of a device drains into block b + 1, b + 2 or b + 3 of the same device and column group, and 16 means the flow leaves toward the next column group.
All inputs are finite; a program needn't handle non-finite values.
Results may differ from the reference program's by a relative error of at most 0.0005.
Values may be sent and summed in bfloat16 or wider, within the bound.
A program may use at most 64 MiB of HBM per device.

```python
import math
import jax
import jax.numpy as jnp
from jax import lax

FAC = 16
VARS = 7
SEG = 128
SWEEPS = 8
NBLK = 16
TC = 256
NX = 2048
NY = 4096
CR = 128
CC = 256
BR = 16
BLOCKS = 128
SEGS = 2048
N_ROW = 8
N_COL = 16


def draw_mfd_weights(key, part):
    first_key, second_key = jax.random.split(key)
    shares = jax.random.uniform(first_key, (8, NX, NY), jnp.float32, 0.05, 1.0)
    totals = jax.random.uniform(second_key, (NX, NY), jnp.float32, 0.6, 0.95)
    return (shares / jnp.sum(shares, axis=0) * totals).astype(jnp.bfloat16)


def draw_cell_segment(key, part):
    keys = jax.random.split(jax.random.fold_in(key, 17), 6)
    upper = jax.random.randint(keys[0], (NX, NY), 1, SEG + 1, dtype=jnp.int32)
    middle = jax.random.randint(keys[1], (NX, NY), 0, upper, dtype=jnp.int32)
    inner = jax.random.randint(keys[2], (NX, NY), 0, middle + 1, dtype=jnp.int32)
    flat = jax.random.randint(keys[3], (NX, NY), 0, SEG, dtype=jnp.int32)
    picker = jax.random.randint(keys[4], (NX, NY), 0, 4, dtype=jnp.int32)
    label = jnp.where(picker == 0, flat, inner).astype(jnp.int32)
    order = jax.random.permutation(keys[5], jnp.arange(SEG, dtype=jnp.int32)).astype(jnp.int32)
    return order[label].astype(jnp.int32)


def draw_route_inverse(key, part):
    columns = SEGS // SEG
    samples = jax.random.uniform(key, (BLOCKS, columns, SEG, SEG), jnp.float32, 0.05, 1.0)
    peaked = samples ** 8
    mixing = peaked / jnp.sum(peaked, axis=2, keepdims=True)
    identity = jnp.eye(SEG, dtype=jnp.float32)
    return (0.2 * identity + 0.8 * mixing).reshape(BLOCKS, SEGS, SEG)


def draw_downstream(key, part):
    columns = SEGS // SEG
    position = jnp.arange(BLOCKS, dtype=jnp.int32) % NBLK
    steps_ahead = jax.random.randint(key, (BLOCKS, columns), 1, 4, dtype=jnp.int32)
    return jnp.minimum(position[:, None] + steps_ahead, NBLK).astype(jnp.int32)


def steps_of(own_key, extent, cuts, least, top_value):
    level, own = 1.0, jax.random.fold_in(own_key, 6)
    for dim, blocks in cuts:
        heights = jnp.exp(jax.random.uniform(jax.random.fold_in(own, dim), (blocks,), jnp.float32, least / len(cuts), top_value / len(cuts)))
        level = level * jnp.repeat(heights, extent[dim] // blocks).reshape([-1 if axis == dim else 1 for axis in range(len(extent))])
    return level


def setup_inputs(seed: int = 0) -> dict:
    key_of = jax.random.split(jax.random.key(seed), 13)
    return {
        "wrf_forcing": jnp.clip(1.0 * jax.random.uniform(key_of[0], (VARS, CR, CC), jnp.float32) ** steps_of(key_of[0], (VARS, CR, CC), ((1, 128),), -0.2, 0.2), 0.0, 1.0),
        "ground_height_km": jnp.clip(0.2 + 2.8 * jax.random.uniform(key_of[1], (NX, NY), jnp.float32) ** steps_of(key_of[1], (NX, NY), ((0, 8), (1, 16)), -0.2, 0.2), 0.2, 3.0),
        "reflected_share": jnp.clip(0.35 + 0.5 * jax.random.uniform(key_of[2], (NX, NY), jnp.float32) ** steps_of(key_of[2], (NX, NY), ((0, 8), (1, 16)), -0.2, 0.2), 0.35, 0.85),
        "snow_water": jnp.clip(6.0 * jax.random.uniform(key_of[3], (NX, NY), jnp.float32) ** steps_of(key_of[3], (NX, NY), ((0, 8), (1, 16)), -0.2, 0.2), 0.0, 6.0),
        "soil_water": jnp.clip(1.0 + 7.0 * jax.random.uniform(key_of[4], (NX, NY), jnp.float32) ** steps_of(key_of[4], (NX, NY), ((0, 8), (1, 16)), -0.2, 0.2), 1.0, 8.0),
        "saturated": jnp.clip(0.5 + 3.5 * jax.random.uniform(key_of[5], (NX, NY), jnp.float32) ** steps_of(key_of[5], (NX, NY), ((0, 8), (1, 16)), -0.2, 0.2), 0.5, 4.0),
        "release_rate": jnp.clip(jnp.exp(math.log(0.3) - 1.7917595 * jax.random.uniform(key_of[6], (NX, NY), jnp.float32) ** steps_of(key_of[6], (NX, NY), ((0, 8), (1, 16)), -0.2, 0.2)), 0.05, 0.3),
        "mfd_weights": draw_mfd_weights(jax.random.fold_in(key_of[12], 71), 0),
        "cell_segment": draw_cell_segment(jax.random.fold_in(key_of[12], 71), 0),
        "route_inverse": draw_route_inverse(jax.random.fold_in(key_of[12], 71), 0),
        "transfer": jnp.clip(0.96 + 0.04000002 * jax.random.uniform(key_of[10], (BLOCKS, SEGS), jnp.float32) ** steps_of(key_of[10], (BLOCKS, SEGS), ((0, 8), (1, 16)), -0.2, 0.2), 0.96, 1.0),
        "downstream": draw_downstream(jax.random.fold_in(key_of[12], 71), 0),
    }


OFFSETS = ((-1, -1), (-1, 0), (-1, 1), (0, -1), (0, 1), (1, -1), (1, 0), (1, 1))
precise = lax.Precision.HIGHEST


def interp_matrix(cell_count, coarse):
    cell_index = jnp.arange(cell_count, dtype=jnp.int32)
    numerator = 2 * cell_index + 1 - FAC
    lower_point = numerator // (2 * FAC)
    fraction = (numerator - 2 * FAC * lower_point).astype(jnp.float32) / (2.0 * FAC)
    column = jnp.arange(coarse + 2, dtype=jnp.int32)
    first_weight = (column[None, :] == (lower_point + 1)[:, None]).astype(jnp.float32)
    second = (column[None, :] == (lower_point + 2)[:, None]).astype(jnp.float32)
    return first_weight * (1.0 - fraction)[:, None] + second * fraction[:, None]


def downscale(padded, row_matrix, col_matrix):
    rows_done = jnp.einsum('ik,vkl->vil', row_matrix, padded, precision=precise)
    return jnp.einsum('vil,jl->vij', rows_done, col_matrix, precision=precise)


def energy_balance(meteorological_drivers, ground_height_km, reflected_share, snow_water, soil_water, saturated):
    lowlevel_heat_degree = -10.0 + 20.0 * meteorological_drivers[0] + 6.5 * ((0.5 + 2.0 * meteorological_drivers[6]) - ground_height_km)
    solar_incoming_flux = 0.8 * meteorological_drivers[1]
    thermal_infrared_flux = 0.25 + 0.15 * meteorological_drivers[2]
    deficit = 1.5 * meteorological_drivers[3]
    lowlevel_breeze_rate = 0.5 + 6.0 * meteorological_drivers[4]
    overall_rain_depth = 4.0 * meteorological_drivers[5]
    frozen_fall_depth = overall_rain_depth / (1.0 + jnp.exp(lowlevel_heat_degree / 1.5))
    rainfall = overall_rain_depth - frozen_fall_depth
    heat_gain_budget = solar_incoming_flux * (1.0 - reflected_share) + thermal_infrared_flux - 0.3 + 0.02 * lowlevel_breeze_rate * lowlevel_heat_degree
    melted = jnp.minimum(10.8 * jnp.maximum(heat_gain_budget, 0.0), snow_water + frozen_fall_depth)
    snowpack = (snow_water + frozen_fall_depth) - melted
    wetted = soil_water + rainfall + melted
    evaporation = (0.3 * solar_incoming_flux + 0.2 * deficit * (1.0 + 0.1 * lowlevel_breeze_rate)) * wetted / (wetted + 2.0)
    remaining = wetted - evaporation
    recharge = 0.4 * jnp.maximum(remaining - 6.0, 0.0)
    return snowpack, remaining - recharge, saturated + recharge


def keep_fraction(weights):
    summed = weights[0]
    for direction in range(1, weights.shape[0]):
        summed = summed + weights[direction]
    return 1.0 - summed


def sweeps_whole(storage, release_rate, weights, retained):
    rows_all, cols_all = storage.shape
    drained = jnp.zeros_like(storage)
    for sweep_index in range(SWEEPS):
        outflow = release_rate * storage
        inflow = jnp.zeros_like(storage)
        for direction, (down_row, down_col) in enumerate(OFFSETS):
            flux_term = jnp.pad(weights[direction] * outflow, 1)
            inflow = inflow + flux_term[1 - down_row:1 - down_row + rows_all, 1 - down_col:1 - down_col + cols_all]
        storage = (storage - outflow) + inflow
        drained = drained + retained * outflow
    return storage, drained


def route_blocks(inverse, transfer, drains_into, lateral, entering):
    blocks = inverse.shape[0]
    seg_width = inverse.shape[1]
    carried = jnp.zeros((blocks + 1, seg_width), jnp.float32).at[0].set(entering)
    block_flows = jnp.zeros((blocks, seg_width), jnp.float32)

    def advance(current, carry_state):
        carried, block_flows = carry_state
        source = lateral[current] + carried[current]
        outflow = jnp.dot(inverse[current], source, precision=precise)
        target = drains_into[current]
        carried = carried.at[target].add(transfer[current] * outflow)
        block_flows = block_flows.at[current].set(outflow)
        return carried, block_flows

    carried, block_flows = lax.fori_loop(0, blocks, advance, (carried, block_flows))
    return block_flows, carried[blocks]


def lateral_whole(drained, cell_segment):
    shaped = drained.reshape(N_ROW, NBLK, BR, N_COL, TC).transpose(0, 1, 3, 2, 4)
    labels = cell_segment.reshape(N_ROW, NBLK, BR, N_COL, TC).transpose(0, 1, 3, 2, 4)
    group_base = jnp.arange(N_ROW * NBLK * N_COL, dtype=jnp.int32).reshape(N_ROW, NBLK, N_COL, 1, 1)
    flat_ids = (group_base * SEG + labels).reshape(-1).astype(jnp.int32)
    totals = jax.ops.segment_sum(shaped.reshape(-1), flat_ids, num_segments=N_ROW * NBLK * N_COL * SEG)
    return 0.001 * totals.reshape(N_ROW, NBLK, N_COL, SEG)


def column_step(entering, pieces):
    inverse_here, transfer_here, drains_here, lateral_here = pieces
    block_flows, leaving = jax.vmap(route_blocks)(inverse_here, transfer_here, drains_here, lateral_here, entering)
    return leaving, block_flows


def reference(wrf_forcing, ground_height_km, reflected_share, snow_water, soil_water, saturated, release_rate, mfd_weights, cell_segment, route_inverse, transfer, downstream):
    padded = jnp.pad(wrf_forcing, ((0, 0), (1, 1), (1, 1)), mode="edge")
    meteorological_drivers = downscale(padded, interp_matrix(NX, CR), interp_matrix(NY, CC))
    snowpack, soil_moisture, storage = energy_balance(meteorological_drivers, ground_height_km, reflected_share, snow_water, soil_water, saturated)
    weights = mfd_weights.astype(jnp.float32)
    retained = keep_fraction(weights)
    groundwater, drained = sweeps_whole(storage, release_rate, weights, retained)
    lateral = lateral_whole(drained, cell_segment).transpose(2, 0, 1, 3)
    inverse_cols = route_inverse.reshape(N_ROW, NBLK, N_COL, SEG, SEG).transpose(2, 0, 1, 3, 4)
    transfer_cols = transfer.reshape(N_ROW, NBLK, N_COL, SEG).transpose(2, 0, 1, 3)
    drains_cols = downstream.reshape(N_ROW, NBLK, N_COL).transpose(2, 0, 1)
    start = jnp.zeros((N_ROW, SEG), jnp.float32)
    leaving, block_flows = lax.scan(column_step, start, (inverse_cols, transfer_cols, drains_cols, lateral))
    channel_flow = block_flows.transpose(1, 2, 0, 3).reshape(N_ROW * NBLK, N_COL * SEG)
    return snowpack, soil_moisture, groundwater, channel_flow
```

```python
import functools

import jax
import jax.numpy as jnp
from jax import lax
from jax.experimental import pallas as pl
from jax.experimental.pallas import tpu as pltpu
from jax.sharding import PartitionSpec as P

MESH = pl.DeviceIdType.MESH
F32, BF16 = jnp.float32, jnp.bfloat16

FAC = 16
VARS = 7
SEG = 128
SWEEPS = 8
NBLK = 16
BR = 16
TILE = 256
RIM = 8
TOP = 16
ROWS = TILE + 32
OFFSETS = ((-1, -1), (-1, 0), (-1, 1), (0, -1), (0, 1), (1, -1), (1, 0), (1, 1))
GROUND, REFLECTED, SNOW, SOIL, STORE, RATE, WEIGHT = range(7)
ARRAYS = 14


def split(x):
    high = x.astype(BF16)
    return high, (x - high.astype(F32)).astype(BF16)


def nn(a, b):
    return lax.dot_general(a, b, (((1,), (0,)), ((), ())), preferred_element_type=F32)


def nt(a, b):
    return lax.dot_general(a, b, (((1,), (1,)), ((), ())), preferred_element_type=F32)


def product(dot, a, b_high, b_low):
    a_high, a_low = split(a)
    return dot(a_high, b_high) + (dot(a_low, b_high) + dot(a_high, b_low))


def iota(shape, dim):
    return lax.broadcasted_iota(jnp.int32, shape, dim)


def kernel(
    n_row,
    n_col,
    forcing,
    ground,
    reflected,
    snow_water,
    soil_water,
    saturated,
    release,
    mfd,
    segment,
    route,
    transfer,
    downstream,
    snow_out,
    soil_out,
    ground_out,
    flow_out,
    ext,
    wb,
    seg,
    inv,
    wmat,
    fmat,
    mats,
    tmat,
    ahot,
    bhot,
    hot,
    strips,
    rims,
    mine,
    rows_in,
    coarse,
    outflow,
    drained,
    retained,
    trans,
    lat,
    flow0,
    gsend,
    gin,
    load_sem,
    store_sem,
    fsend,
    frecv,
    ssend,
    srecv,
    rsend,
    rrecv,
    msend,
    mrecv,
    gsend_sem,
    grecv,
):
    r, c = lax.axis_index("row"), lax.axis_index("col")
    has_up, has_down = r > 0, r < n_row - 1
    has_left, has_right = c > 0, c < n_col - 1

    barrier = pltpu.get_barrier_semaphore()

    def greet(row, col):
        pl.semaphore_signal(barrier, inc=1, device_id=(row, col), device_id_type=MESH)

    @pl.loop(1, n_col)
    def _(d):
        greet(r, lax.rem(c + d, n_col))

    @pl.when(has_up)
    def _():
        greet(r - 1, c)
        greet(r - 1, n_col - 1)

    @pl.when(has_down)
    def _():
        greet(r + 1, c)
        greet(r + 1, 0)

    loads = [pltpu.make_async_copy(route, inv, load_sem.at[0])]
    loads.append(pltpu.make_async_copy(mfd, wb, load_sem.at[1]))
    n = 2
    for k, ref in enumerate((ground, reflected, snow_water, soil_water, saturated, release)):
        for t in range(2):
            loads.append(
                pltpu.make_async_copy(
                    ref.at[:, pl.ds(128 * t, 128)],
                    ext.at[k, t, pl.ds(TOP, TILE), :],
                    load_sem.at[n],
                )
            )
            n += 1
    for t in range(2):
        loads.append(
            pltpu.make_async_copy(segment.at[:, pl.ds(128 * t, 128)], seg.at[t], load_sem.at[n + t])
        )
    for copy in loads[1:]:
        copy.start()
    loads[0].start()

    eye = (iota((SEG, SEG), 0) == iota((SEG, SEG), 1)).astype(F32)
    wmat[NBLK] = eye
    fmat[0] = jnp.zeros((SEG, SEG), F32)
    fmat[1] = jnp.zeros((SEG, SEG), F32)
    fmat[2] = eye
    trans[0:3, :] = jnp.ones((3, SEG), F32)
    trans[3 : 3 + NBLK, :] = transfer[...]
    flow0[0:3, :] = jnp.zeros((3, SEG), F32)
    for v in range(VARS):
        mine[v : v + 1, :] = forcing[v]
    mine[VARS : VARS + 1, :] = jnp.zeros((1, mine.shape[1]), F32)
    rows_in[c + 1] = mine[...]

    @pl.when(jnp.logical_not(has_up))
    def _():
        ext[:, :, pl.ds(TOP - RIM, RIM), :] = jnp.zeros((ARRAYS, 3, RIM, 128), F32)

    @pl.when(jnp.logical_not(has_down))
    def _():
        ext[:, :, pl.ds(TOP + TILE, RIM), :] = jnp.zeros((ARRAYS, 3, RIM, 128), F32)

    pl.semaphore_wait(
        barrier,
        n_col
        - 1
        + has_up.astype(jnp.int32)
        + has_down.astype(jnp.int32)
        + jnp.where(jnp.logical_and(c == n_col - 1, has_down), n_col, 0)
        + jnp.where(jnp.logical_and(c == 0, has_up), n_col, 0),
    )

    def forcing_copy(row, col, slot, sem):
        return pltpu.make_async_remote_copy(
            src_ref=mine,
            dst_ref=rows_in.at[slot],
            send_sem=fsend.at[sem],
            recv_sem=frecv.at[slot],
            device_id=(row, col),
            device_id_type=MESH,
        )

    @pl.loop(1, n_col)
    def _(d):
        forcing_copy(r, lax.rem(c + d, n_col), c + 1, d).start()

    sends_down = jnp.logical_and(c == n_col - 1, has_down)
    sends_up = jnp.logical_and(c == 0, has_up)

    @pl.when(sends_down)
    def _():
        @pl.loop(0, n_col)
        def _(d):
            forcing_copy(r + 1, d, 0, n_col + d).start()

    @pl.when(sends_up)
    def _():
        @pl.loop(0, n_col)
        def _(d):
            forcing_copy(r - 1, d, n_col + 1, 2 * n_col + d).start()

    for copy in loads[1:-2]:
        copy.wait()

    step_rows = 32

    @pl.loop(0, TILE // step_rows)
    def _(i):
        here = pl.ds(pl.multiple_of(i * step_rows, step_rows), step_rows)
        there = pl.ds(pl.multiple_of(TOP + i * step_rows, 8), step_rows)
        lane = iota((step_rows, 128), 1)
        left = jnp.zeros((step_rows, 128), F32)
        right = jnp.zeros((step_rows, 128), F32)
        total = [None, None]
        for k in range(ARRAYS):
            pair = []
            for t in range(2):
                if k < WEIGHT:
                    x = ext[k, t, there, :]
                else:
                    x = wb[k - WEIGHT, here, pl.ds(128 * t, 128)].astype(F32)
                    ext[k, t, there, :] = x
                    total[t] = x if total[t] is None else total[t] + x
                pair.append(x)
            place = jnp.logical_and(lane >= 8 * k, lane < 8 * k + 8)
            left = jnp.where(place, pltpu.roll(pair[0], 8 * k, 1) if k else pair[0], left)
            right = jnp.where(place, pltpu.roll(pair[1], (8 * k + 8) % 128, 1), right)
        for t in range(2):
            retained[t, there, :] = 1.0 - total[t]
        strips[0, here, :] = left
        strips[1, here, :] = right

    def strip_copy(side, col):
        return pltpu.make_async_remote_copy(
            src_ref=strips.at[side],
            dst_ref=rims.at[side],
            send_sem=ssend.at[side],
            recv_sem=srecv.at[side],
            device_id=(r, col),
            device_id_type=MESH,
        )

    @pl.when(has_left)
    def _():
        strip_copy(0, c - 1).start()

    @pl.when(has_right)
    def _():
        strip_copy(1, c + 1).start()

    loads[0].wait()

    def drains_here(block, back):
        before = block - back
        drains = downstream[jnp.maximum(before, 0), 0] == block
        first = jnp.logical_and(block == 0, back == 1)
        return jnp.where(before >= 0, drains, first).astype(F32)

    def responses(start, stop):
        @pl.loop(start, stop)
        def _(i):
            b = NBLK - 1 - i
            high, low = split(inv[b])
            later = wmat[downstream[b, 0]] * trans[pl.ds(b + 3, 1), :]
            wmat[b] = product(nn, later, high, low)
            high, low = split(inv[i])
            carried = jnp.zeros((SEG, SEG), F32)
            for back in range(1, 4):
                share = trans[pl.ds(i + 3 - back, 1), :] * drains_here(i, back)
                carried = carried + fmat[i + 3 - back] * share
            fmat[i + 3] = product(nt, carried, high, low)

    responses(0, 8)

    @pl.when(has_right)
    def _():
        strip_copy(0, c + 1).wait_recv()

    @pl.when(has_left)
    def _():
        strip_copy(1, c - 1).wait_recv()

    @pl.loop(0, TILE // step_rows)
    def _(i):
        here = pl.ds(pl.multiple_of(i * step_rows, step_rows), step_rows)
        there = pl.ds(pl.multiple_of(TOP + i * step_rows, 8), step_rows)
        lane = iota((step_rows, 128), 1)
        at_right = jnp.logical_and(lane < RIM, has_right)
        at_left = jnp.logical_and(lane >= 128 - RIM, has_left)
        from_right = rims[0, here, :]
        from_left = rims[1, here, :]
        for k in range(ARRAYS):
            a = pltpu.roll(from_right, (128 - 8 * k) % 128, 1) if k else from_right
            b = pltpu.roll(from_left, (120 - 8 * k) % 128, 1)
            ext[k, 2, there, :] = jnp.where(at_right, a, jnp.where(at_left, b, 0.0))

    def row_copy(side, row):
        source, target = (TOP, TOP + TILE) if side == 0 else (TOP + TILE - RIM, TOP - RIM)
        return pltpu.make_async_remote_copy(
            src_ref=ext.at[:, :, pl.ds(source, RIM), :],
            dst_ref=ext.at[:, :, pl.ds(target, RIM), :],
            send_sem=rsend.at[side],
            recv_sem=rrecv.at[side],
            device_id=(row, c),
            device_id_type=MESH,
        )

    @pl.when(has_up)
    def _():
        row_copy(0, r - 1).start()

    @pl.when(has_down)
    def _():
        row_copy(1, r + 1).start()

    responses(8, NBLK)

    def matrix_copy(col, slot):
        return pltpu.make_async_remote_copy(
            src_ref=wmat.at[0],
            dst_ref=mats.at[slot],
            send_sem=msend.at[col],
            recv_sem=mrecv.at[slot],
            device_id=(r, col),
            device_id_type=MESH,
        )

    @pl.when(has_left)
    def _():
        @pl.loop(c + 1, n_col)
        def _(col):
            matrix_copy(col, c).start()

    for copy in loads[-2:]:
        copy.wait()

    @pl.loop(0, NBLK)
    def _(b):
        target = pl.ds(pl.multiple_of(b * 16, 16), 16)
        low = iota((16, 128), 0)
        for i in range(BR):
            for t in range(2):
                same = jnp.bitwise_and(seg[t, pl.ds(b * BR + i, 1), :], 15) == low
                bhot[i, target, pl.ds(128 * t, 128)] = jnp.where(same, 1.0, 0.0).astype(BF16)

    @pl.loop(1, n_col)
    def _(d):
        forcing_copy(r, c, lax.rem(c + d, n_col) + 1, 0).wait_recv()

    @pl.when(has_up)
    def _():
        forcing_copy(r, c, 0, 0).wait_recv()

    @pl.when(has_down)
    def _():
        forcing_copy(r, c, n_col + 1, 0).wait_recv()

    @pl.when(jnp.logical_not(has_up))
    def _():
        rows_in[0] = rows_in[1]

    @pl.when(jnp.logical_not(has_down))
    def _():
        rows_in[n_col + 1] = rows_in[n_col]

    cells = rows_in.shape[2]
    lanes = iota((cells, 384), 1)
    column = jnp.where(lanes < 320, lanes, lanes - 384) + c * TILE
    numerator = 2 * column + 1 - FAC
    point = lax.shift_right_arithmetic(numerator, 5)
    fraction = (numerator - 2 * FAC * point).astype(F32) * (1.0 / (2 * FAC))
    place = iota((cells, 384), 0)
    first = jnp.clip(point, 0, cells - 1)
    second = jnp.clip(point + 1, 0, cells - 1)
    spread = (
        jnp.where(place == first, 1.0 - fraction, 0.0) + jnp.where(place == second, fraction, 0.0)
    ).astype(BF16)
    points = rows_in[...].reshape((n_col + 2) * 8, cells)
    high, rest = split(points)
    middle, low = split(points - high.astype(F32))
    wide = nn(high, spread) + (nn(middle, spread) + nn(low, spread))
    for t in range(3):
        coarse[t] = wide[:, 128 * t : 128 * t + 128]

    @pl.when(has_up)
    def _():
        row_copy(0, r - 1).wait_send()
        row_copy(1, r - 1).wait_recv()

    @pl.when(has_down)
    def _():
        row_copy(1, r + 1).wait_send()
        row_copy(0, r + 1).wait_recv()

    outflow[0, :, 0 : TOP - RIM, :] = jnp.zeros((3, TOP - RIM, 128), F32)
    outflow[1, :, 0 : TOP - RIM, :] = jnp.zeros((3, TOP - RIM, 128), F32)
    outflow[0, :, TOP + TILE + RIM :, :] = jnp.zeros((3, RIM, 128), F32)
    outflow[1, :, TOP + TILE + RIM :, :] = jnp.zeros((3, RIM, 128), F32)

    @pl.loop(0, TILE // FAC + 1)
    def _(k):
        rows = pl.ds(pl.multiple_of(TOP - RIM + FAC * k, 8), FAC)
        part = (2 * iota((FAC, 128), 0) + 1).astype(F32) * (1.0 / (2 * FAC))
        for t in range(3):
            v = []
            for var in range(VARS):
                above = coarse[t, pl.ds(k * 8 + var, 1), :]
                below = coarse[t, pl.ds(k * 8 + 8 + var, 1), :]
                v.append(above * (1.0 - part) + below * part)
            heat = -10.0 + 20.0 * v[0] + 6.5 * ((0.5 + 2.0 * v[6]) - ext[GROUND, t, rows, :])
            solar = 0.8 * v[1]
            thermal = 0.25 + 0.15 * v[2]
            deficit = 1.5 * v[3]
            breeze = 0.5 + 6.0 * v[4]
            rain = 4.0 * v[5]
            frozen = rain / (1.0 + jnp.exp(heat / 1.5))
            liquid = rain - frozen
            budget = (
                solar * (1.0 - ext[REFLECTED, t, rows, :]) + thermal - 0.3 + 0.02 * breeze * heat
            )
            pack = ext[SNOW, t, rows, :] + frozen
            melted = jnp.minimum(10.8 * jnp.maximum(budget, 0.0), pack)
            wetted = ext[SOIL, t, rows, :] + liquid + melted
            evaporation = (
                (0.3 * solar + 0.2 * deficit * (1.0 + 0.1 * breeze)) * wetted / (wetted + 2.0)
            )
            remaining = wetted - evaporation
            recharge = 0.4 * jnp.maximum(remaining - 6.0, 0.0)
            storage = ext[STORE, t, rows, :] + recharge
            ext[STORE, t, rows, :] = storage
            outflow[0, t, rows, :] = ext[RATE, t, rows, :] * storage
            if t < 2:
                ext[SNOW, t, rows, :] = pack - melted
                ext[SOIL, t, rows, :] = remaining - recharge
                drained[t, rows, :] = jnp.zeros((FAC, 128), F32)

    outs = []
    for k, (index, ref) in enumerate(((SNOW, snow_out), (SOIL, soil_out), (STORE, ground_out))):
        outs.append(
            [
                pltpu.make_async_copy(
                    ext.at[index, t, pl.ds(TOP, TILE), :],
                    ref.at[:, pl.ds(128 * t, 128)],
                    store_sem.at[2 * k + t],
                )
                for t in range(2)
            ]
        )
    for copy in outs[0] + outs[1]:
        copy.start()

    @pl.loop(0, SWEEPS)
    def _(sweep):
        now = lax.rem(sweep, 2)

        @pl.loop(0, (TILE + 2 * RIM) // 16)
        def _(q):
            base = TOP - RIM + 16 * q
            rows = pl.ds(pl.multiple_of(base, 8), 16)
            lane = iota((16, 128), 1)
            sums = {-1: [], 0: [], 1: []}
            middle = []
            for t in range(3):
                parts = {-1: None, 0: None, 1: None}
                for down_row in (-1, 0, 1):
                    at = rows if down_row == 0 else pl.ds(base - down_row, 16)
                    out = outflow[now, t, at, :]
                    if down_row == 0:
                        middle.append(out)
                    for direction, (dr, dc) in enumerate(OFFSETS):
                        if dr == down_row:
                            term = ext[WEIGHT + direction, t, at, :] * out
                            parts[dc] = term if parts[dc] is None else parts[dc] + term
                for dc in (-1, 0, 1):
                    sums[dc].append(parts[dc])
            east = [pltpu.roll(x, 1, 1) for x in sums[1]]
            west = [pltpu.roll(x, 127, 1) for x in sums[-1]]
            for t in range(3):
                inflow = (
                    sums[0][t]
                    + jnp.where(lane == 0, east[(t + 2) % 3], east[t])
                    + jnp.where(lane == 127, west[(t + 1) % 3], west[t])
                )
                storage = (ext[STORE, t, rows, :] - middle[t]) + inflow
                ext[STORE, t, rows, :] = storage
                outflow[1 - now, t, rows, :] = ext[RATE, t, rows, :] * storage
                if t < 2:
                    drained[t, rows, :] = drained[t, rows, :] + retained[t, rows, :] * middle[t]

    for copy in outs[2]:
        copy.start()

    @pl.loop(0, NBLK)
    def _(b):
        target = pl.ds(pl.multiple_of(b * 16, 16), 16)
        top = iota((8, 128), 0)
        for i in range(BR):
            for t in range(2):
                lanes = pl.ds(128 * t, 128)
                label = seg[t, pl.ds(b * BR + i, 1), :]
                value = drained[t, pl.ds(TOP + b * BR + i, 1), :]
                same = lax.shift_right_logical(label, 4) == top
                kept = jnp.where(same, value, 0.0)
                high = kept.astype(BF16).astype(F32)
                both = jnp.concatenate([high, kept - high], axis=0)
                ahot[i, target, lanes] = both.astype(BF16)

    hot[...] = jnp.zeros((2, TILE, 128), F32)

    @pl.loop(0, BR)
    def _(i):
        a = ahot[i]
        for t in range(2):
            hot[t] = hot[t] + nt(a, bhot[i, 128 * t : 128 * t + 128, :])

    lane = iota((8, 128), 1)
    group = lax.shift_right_logical(lane, 4)
    for b in range(NBLK):
        t = b // 8
        x = hot[t, b * 16 : b * 16 + 8, :] + hot[t, b * 16 + 8 : b * 16 + 16, :]
        x = jnp.where(group == b % 8, x, 0.0)
        for shift in (16, 32, 64):
            x = x + pltpu.roll(x, shift, 1)
        x = jnp.where(group == iota((8, 128), 0), x, 0.0)
        lat[b : b + 1, :] = 0.001 * jnp.sum(x, axis=0, keepdims=True)

    def to_row(matrix):
        column = jnp.sum(matrix, axis=1, keepdims=True)
        same = iota((SEG, SEG), 0) == iota((SEG, SEG), 1)
        return jnp.sum(jnp.where(same, column, 0.0), axis=0, keepdims=True)

    def own(b, total):
        return total + wmat[b] * lat[pl.ds(b, 1), :]

    leaving = to_row(lax.fori_loop(0, NBLK, own, jnp.zeros((SEG, SEG), F32)))
    gsend[...] = jnp.broadcast_to(leaving, (8, SEG))

    def leaving_copy(col, slot):
        return pltpu.make_async_remote_copy(
            src_ref=gsend,
            dst_ref=gin.at[slot],
            send_sem=gsend_sem.at[col],
            recv_sem=grecv.at[slot],
            device_id=(r, col),
            device_id_type=MESH,
        )

    @pl.loop(c + 1, n_col)
    def _(col):
        leaving_copy(col, c).start()

    @pl.loop(1, c)
    def _(slot):
        matrix_copy(c, slot).wait_recv()

    tmat[0] = (iota((SEG, SEG), 0) == iota((SEG, SEG), 1)).astype(F32)

    @pl.loop(0, NBLK)
    def _(b):
        high, low = split(mats[jnp.maximum(c - 1 - b, 0)])
        tmat[b + 1] = product(nn, tmat[b], high, low)
        source = lat[pl.ds(b, 1), :]
        for back in range(1, 4):
            share = trans[pl.ds(b + 3 - back, 1), :] * jnp.where(
                b - back >= 0, drains_here(b, back), 0.0
            )
            source = source + share * flow0[pl.ds(b + 3 - back, 1), :]
        flow0[pl.ds(b + 3, 1), :] = to_row(inv[b] * source)

    @pl.loop(0, c)
    def _(slot):
        leaving_copy(c, slot).wait_recv()

    def enter(k, total):
        return total + tmat[k] * gin[c - 1 - k, 0:1, :]

    total = lax.fori_loop(0, c, enter, jnp.zeros((SEG, SEG), F32))
    entering = jnp.sum(total, axis=1, keepdims=True)

    @pl.loop(0, NBLK)
    def _(b):
        extra = jnp.sum(fmat[b + 3] * entering, axis=0, keepdims=True)
        flow_out[pl.ds(b, 1), :] = flow0[pl.ds(b + 3, 1), :] + extra

    for pair in outs:
        for copy in pair:
            copy.wait()

    @pl.loop(1, n_col)
    def _(d):
        forcing_copy(r, c, 0, d).wait_send()

    @pl.when(sends_down)
    def _():
        @pl.loop(0, n_col)
        def _(d):
            forcing_copy(r, c, 0, n_col + d).wait_send()

    @pl.when(sends_up)
    def _():
        @pl.loop(0, n_col)
        def _(d):
            forcing_copy(r, c, 0, 2 * n_col + d).wait_send()

    @pl.when(has_left)
    def _():
        strip_copy(0, c - 1).wait_send()

        @pl.loop(c + 1, n_col)
        def _(col):
            matrix_copy(col, c).wait_send()

    @pl.when(has_right)
    def _():
        strip_copy(1, c + 1).wait_send()

    @pl.loop(c + 1, n_col)
    def _(col):
        leaving_copy(col, c).wait_send()


def per_device(n_row, n_col, forcing, *args):
    cells = forcing.shape[2]
    any_space = pl.BlockSpec(memory_space=pl.ANY)
    vmem = pl.BlockSpec(memory_space=pltpu.VMEM)
    smem = pl.BlockSpec(memory_space=pltpu.SMEM)
    tile = jax.ShapeDtypeStruct((TILE, TILE), F32)
    dma = pltpu.SemaphoreType.DMA
    return pl.pallas_call(
        functools.partial(kernel, n_row, n_col),
        out_shape=(tile, tile, tile, jax.ShapeDtypeStruct((NBLK, SEG), F32)),
        in_specs=[vmem] + [any_space] * 9 + [vmem, smem],
        out_specs=(any_space, any_space, any_space, vmem),
        scratch_shapes=[
            pltpu.VMEM((ARRAYS, 3, ROWS, 128), F32),
            pltpu.VMEM((8, TILE, TILE), BF16),
            pltpu.VMEM((2, TILE, 128), jnp.int32),
            pltpu.VMEM((NBLK, SEG, SEG), F32),
            pltpu.VMEM((NBLK + 1, SEG, SEG), F32),
            pltpu.VMEM((NBLK + 3, SEG, SEG), F32),
            pltpu.VMEM((n_col, SEG, SEG), F32),
            pltpu.VMEM((NBLK + 1, SEG, SEG), F32),
            pltpu.VMEM((BR, TILE, TILE), BF16),
            pltpu.VMEM((BR, TILE, TILE), BF16),
            pltpu.VMEM((2, TILE, 128), F32),
            pltpu.VMEM((2, TILE, 128), F32),
            pltpu.VMEM((2, TILE, 128), F32),
            pltpu.VMEM((8, cells), F32),
            pltpu.VMEM((n_col + 2, 8, cells), F32),
            pltpu.VMEM((3, (n_col + 2) * 8, 128), F32),
            pltpu.VMEM((2, 3, ROWS, 128), F32),
            pltpu.VMEM((2, ROWS, 128), F32),
            pltpu.VMEM((2, ROWS, 128), F32),
            pltpu.VMEM((24, SEG), F32),
            pltpu.VMEM((NBLK, SEG), F32),
            pltpu.VMEM((24, SEG), F32),
            pltpu.VMEM((8, SEG), F32),
            pltpu.VMEM((n_col, 8, SEG), F32),
            dma((16,)),
            dma((6,)),
            dma((3 * n_col,)),
            dma((n_col + 2,)),
            dma((2,)),
            dma((2,)),
            dma((2,)),
            dma((2,)),
            dma((n_col,)),
            dma((n_col,)),
            dma((n_col,)),
            dma((n_col,)),
        ],
        compiler_params=pltpu.CompilerParams(collective_id=0, has_side_effects=True),
        name="hydrology",
    )(forcing, *args)


def solution(mesh):
    n_row, n_col = mesh.shape["row"], mesh.shape["col"]
    tiles = P("row", "col")
    placed = (
        P(None, ("row", "col"), None),
        *(tiles for _ in range(6)),
        P(None, "row", "col"),
        tiles,
        P("row", "col", None),
        tiles,
        tiles,
    )
    return jax.shard_map(
        functools.partial(per_device, n_row, n_col),
        mesh=mesh,
        in_specs=placed,
        out_specs=(tiles, tiles, tiles, tiles),
        check_vma=False,
    )
```

```python
import functools

import jax
import jax.numpy as jnp
from jax import lax
from jax.experimental import pallas as pl
from jax.experimental.pallas import tpu as pltpu
from jax.sharding import PartitionSpec as P

MESH = pl.DeviceIdType.MESH
F32, BF16 = jnp.float32, jnp.bfloat16

FAC = 16
VARS = 7
SEG = 128
SWEEPS = 8
NBLK = 16
BR = 16
TILE = 256
RIM = 8
TOP = 16
ROWS = TILE + 32
OFFSETS = ((-1, -1), (-1, 0), (-1, 1), (0, -1), (0, 1), (1, -1), (1, 0), (1, 1))
GROUND, REFLECTED, SNOW, SOIL, STORE, RATE, WEIGHT = range(7)
ARRAYS = 14
MELT = 10.8
SIDE = 4


def split(x):
    high = x.astype(BF16)
    return high, (x - high.astype(F32)).astype(BF16)


def nn(a, b):
    return lax.dot_general(a, b, (((1,), (0,)), ((), ())), preferred_element_type=F32)


def nt(a, b):
    return lax.dot_general(a, b, (((1,), (1,)), ((), ())), preferred_element_type=F32)


def both(x, axis):
    return jnp.concatenate(split(x), axis=axis)


def product(a, b):
    right = both(b, 1)
    wide = nn(both(a, 1), jnp.concatenate([right, right], axis=0))
    return wide[:, :SEG] + wide[:, SEG:]


def product_nt(a, b):
    right = both(b, 0)
    wide = nt(both(a, 1), jnp.concatenate([right, right], axis=1))
    return wide[:, :SEG] + wide[:, SEG:]


def iota(shape, dim):
    return lax.broadcasted_iota(jnp.int32, shape, dim)


def kernel(
    n_row,
    n_col,
    forcing,
    ground,
    reflected,
    snow_water,
    soil_water,
    saturated,
    release,
    mfd,
    segment,
    route,
    transfer,
    downstream,
    snow_out,
    soil_out,
    ground_out,
    flow_out,
    ext,
    wb,
    seg,
    inv,
    wmat,
    fmat,
    mats,
    after,
    tmat,
    gmats,
    ahot,
    bhot,
    hot,
    strips,
    rims,
    wrim,
    mine,
    rows_in,
    spread,
    coarse,
    first_out,
    second_out,
    drained,
    retained,
    trans,
    lat,
    flow0,
    gsend,
    gin,
    load_sem,
    fsend,
    frecv,
    ssend,
    srecv,
    rsend,
    rrecv,
    msend,
    mrecv,
    qsend,
    qrecv,
    gsend_sem,
    grecv,
):
    r, c = lax.axis_index("row"), lax.axis_index("col")
    has_up, has_down = r > 0, r < n_row - 1
    has_left, has_right = c > 0, c < n_col - 1

    barrier = pltpu.get_barrier_semaphore()

    def greet(row, col):
        pl.semaphore_signal(barrier, inc=1, device_id=(row, col), device_id_type=MESH)

    @pl.loop(1, n_col)
    def _(d):
        greet(r, lax.rem(c + d, n_col))

    @pl.when(has_up)
    def _():
        greet(r - 1, c)
        greet(r - 1, n_col - 1)

        @pl.when(has_left)
        def _():
            greet(r - 1, c - 1)

        @pl.when(has_right)
        def _():
            greet(r - 1, c + 1)

    @pl.when(has_down)
    def _():
        greet(r + 1, c)
        greet(r + 1, 0)

        @pl.when(has_left)
        def _():
            greet(r + 1, c - 1)

        @pl.when(has_right)
        def _():
            greet(r + 1, c + 1)

    for k, ref in enumerate((ground, reflected, snow_water, soil_water, saturated, release)):
        for t in range(2):
            pltpu.make_async_copy(
                ref.at[:, pl.ds(128 * t, 128)], ext.at[k, t, pl.ds(TOP, TILE), :], load_sem.at[0]
            ).start()
    load_weights = pltpu.make_async_copy(mfd, wb, load_sem.at[1])
    load_weights.start()
    load_route = pltpu.make_async_copy(route, inv, load_sem.at[2])
    load_route.start()
    for t in range(2):
        pltpu.make_async_copy(
            segment.at[:, pl.ds(128 * t, 128)], seg.at[t], load_sem.at[3]
        ).start()

    eye = (iota((SEG, SEG), 0) == iota((SEG, SEG), 1)).astype(F32)
    wmat[NBLK] = eye
    after[0] = eye
    tmat[0] = eye
    mats[SIDE] = jnp.zeros((SEG, SEG), F32)
    gmats[n_col // SIDE] = jnp.zeros((SEG, SEG), F32)
    gin[c] = jnp.zeros((8, SEG), F32)
    gsend[...] = jnp.zeros((8, SEG), F32)
    fmat[0] = jnp.zeros((SEG, SEG), F32)
    fmat[1] = jnp.zeros((SEG, SEG), F32)
    fmat[2] = eye
    trans[0:3, :] = jnp.ones((3, SEG), F32)
    trans[3 : 3 + NBLK, :] = transfer[...]
    flow0[0:3, :] = jnp.zeros((3, SEG), F32)
    low_half, high_half = c <= n_col // 2, c >= n_col // 2 - 1
    for half in range(2):
        lanes = pl.ds(half * mine.shape[2], mine.shape[2])
        for v in range(VARS):
            mine[half, v : v + 1, :] = forcing[v, :, lanes]
        mine[half, VARS : VARS + 1, :] = jnp.zeros((1, mine.shape[2]), F32)

    @pl.when(jnp.logical_not(low_half))
    def _():
        rows_in[0] = jnp.zeros(rows_in.shape[1:], F32)

    @pl.when(jnp.logical_not(high_half))
    def _():
        rows_in[1] = jnp.zeros(rows_in.shape[1:], F32)

    @pl.when(low_half)
    def _():
        rows_in[0, c + 1] = mine[0]

    @pl.when(high_half)
    def _():
        rows_in[1, c + 1] = mine[1]

    @pl.when(jnp.logical_not(has_up))
    def _():
        ext[:, :, pl.ds(TOP - RIM, RIM), :] = jnp.zeros((ARRAYS, 3, RIM, 128), F32)

    @pl.when(jnp.logical_not(has_down))
    def _():
        ext[:, :, pl.ds(TOP + TILE, RIM), :] = jnp.zeros((ARRAYS, 3, RIM, 128), F32)

    load_weights.wait()
    six = ext.at[pl.ds(0, WEIGHT), pl.ds(0, 2), pl.ds(TOP, TILE), :]
    pltpu.make_async_copy(six, six, load_sem.at[0]).wait()

    step_rows = 64

    def pack_side(side):
        @pl.loop(0, TILE // step_rows)
        def _(i):
            here = pl.ds(pl.multiple_of(i * step_rows, step_rows), step_rows)
            there = pl.ds(pl.multiple_of(TOP + i * step_rows, 8), step_rows)
            lane = iota((step_rows, 128), 1)
            packed = jnp.zeros((step_rows, 128), F32)
            for k in range(ARRAYS):
                if k < WEIGHT:
                    x = ext[k, side, there, :]
                else:
                    x = wb[k - WEIGHT, here, pl.ds(128 * side, 128)].astype(F32)
                shift = (8 * k + 8 * side) % 128
                place = jnp.logical_and(lane >= 8 * k, lane < 8 * k + 8)
                packed = jnp.where(place, pltpu.roll(x, shift, 1) if shift else x, packed)
            strips[side, here, :] = packed

    pack_side(1)

    def strip_copies(side, row_step, row, col):
        source, target, rows = {
            0: (0, RIM, TILE),
            -1: (0, RIM + TILE, RIM),
            1: (TILE - RIM, 0, RIM),
        }[row_step]
        return pltpu.make_async_remote_copy(
            src_ref=strips.at[side, pl.ds(source, rows), :],
            dst_ref=rims.at[side, pl.ds(target, rows), :],
            send_sem=ssend.at[3 * side + row_step + 1],
            recv_sem=srecv.at[3 * side + row_step + 1],
            device_id=(row, col),
            device_id_type=MESH,
        )

    def each_strip(act, sending, sides=(0, 1)):
        for side in sides:
            toward_left = (side == 0) == sending
            there, col = (has_left, c - 1) if toward_left else (has_right, c + 1)
            for row_step in (0, -1, 1):
                ok, row = there, r
                if row_step:
                    toward_up = (row_step == -1) == sending
                    ok = jnp.logical_and(there, has_up if toward_up else has_down)
                    row = r - 1 if toward_up else r + 1

                @pl.when(ok)
                def _():
                    act(strip_copies(side, row_step, row, col))

    pl.semaphore_wait(
        barrier,
        n_col
        - 1
        + (has_up.astype(jnp.int32) + has_down.astype(jnp.int32))
        * (1 + has_left.astype(jnp.int32) + has_right.astype(jnp.int32))
        + jnp.where(jnp.logical_and(c == n_col - 1, has_down), n_col, 0)
        + jnp.where(jnp.logical_and(c == 0, has_up), n_col, 0),
    )

    def forcing_copy(half, row, col, slot, sem):
        return pltpu.make_async_remote_copy(
            src_ref=mine.at[half],
            dst_ref=rows_in.at[half, slot],
            send_sem=fsend.at[2 * sem + half],
            recv_sem=frecv.at[2 * sem + half],
            device_id=(row, col),
            device_id_type=MESH,
        )

    halves = ((0, 0, n_col // 2 + 1), (1, n_col // 2 - 1, n_col))
    sends_down = jnp.logical_and(c == n_col - 1, has_down)
    sends_up = jnp.logical_and(c == 0, has_up)

    @pl.when(sends_down)
    def _():
        for half, start, stop in halves:

            @pl.loop(start, stop)
            def _(d):
                forcing_copy(half, r + 1, d, 0, 1).start()

    @pl.when(sends_up)
    def _():
        for half, start, stop in halves:

            @pl.loop(start, stop)
            def _(d):
                forcing_copy(half, r - 1, d, n_col + 1, 2).start()

    for half, start, stop in halves:

        @pl.loop(start, stop)
        def _(d):
            @pl.when(d != c)
            def _():
                forcing_copy(half, r, d, c + 1, 0).start()

    each_strip(lambda copy: copy.start(), True, (1,))

    def row_copies(side, row):
        source, target = (0, TOP + TILE) if side == 0 else (TILE - RIM, TOP - RIM)

        def remote(src, dst, n):
            return pltpu.make_async_remote_copy(
                src_ref=src,
                dst_ref=dst,
                send_sem=rsend.at[2 * side + n],
                recv_sem=rrecv.at[2 * side + n],
                device_id=(row, c),
                device_id_type=MESH,
            )

        inputs = pl.ds(0, WEIGHT)
        two = pl.ds(0, 2)
        return (
            remote(
                ext.at[inputs, two, pl.ds(TOP + source, RIM), :],
                ext.at[inputs, two, pl.ds(target, RIM), :],
                0,
            ),
            remote(wb.at[:, pl.ds(source, RIM), :], wrim.at[side], 1),
        )

    @pl.when(has_up)
    def _():
        for copy in row_copies(0, r - 1):
            copy.start()

    @pl.when(has_down)
    def _():
        for copy in row_copies(1, r + 1):
            copy.start()

    pack_side(0)
    each_strip(lambda copy: copy.start(), True, (0,))

    load_route.wait()
    pltpu.make_async_copy(seg, seg, load_sem.at[3]).wait()

    def drains_here(block, back):
        before = block - back
        drains = downstream[0, jnp.maximum(before, 0)] == block
        first = jnp.logical_and(block == 0, back == 1)
        return jnp.where(before >= 0, drains, first).astype(F32)

    @pl.loop(0, NBLK)
    def _(i):
        b = NBLK - 1 - i
        later = wmat[downstream[0, b]] * trans[pl.ds(b + 3, 1), :]
        wmat[b] = product(later, inv[b])

        target = pl.ds(pl.multiple_of(i * 16, 16), 16)
        low_part = iota((16, 128), 0)
        for j in range(BR):
            for t in range(2):
                same = jnp.bitwise_and(seg[t, pl.ds(i * BR + j, 1), :], 15) == low_part
                bhot[target, pl.ds(j * TILE + 128 * t, 128)] = jnp.where(same, 1.0, 0.0).astype(
                    BF16
                )

        there = pl.ds(pl.multiple_of(TOP + i * 16, 8), 16)
        for t in range(2):
            kept = None
            for d in range(8):
                x = wb[d, target, pl.ds(128 * t, 128)].astype(F32)
                ext[WEIGHT + d, t, there, :] = x
                kept = x if kept is None else kept + x
            retained[t, there, :] = 1.0 - kept

    across, group = lax.rem(c, SIDE), lax.div(c, SIDE)

    def matrix_copy(to, slot):
        return pltpu.make_async_remote_copy(
            src_ref=wmat.at[0],
            dst_ref=mats.at[slot],
            send_sem=msend.at[to],
            recv_sem=mrecv.at[slot],
            device_id=(r, group * SIDE + to),
            device_id_type=MESH,
        )

    @pl.loop(1, SIDE)
    def _(k):
        matrix_copy(lax.rem(across + k, SIDE), across).start()

    mats[across] = wmat[0]

    cells = 2 * rows_in.shape[3]
    lanes = iota((cells, 384), 1)
    column = jnp.where(lanes < 320, lanes, lanes - 384) + c * TILE
    numerator = 2 * column + 1 - FAC
    point = lax.shift_right_arithmetic(numerator, 5)
    fraction = (numerator - 2 * FAC * point).astype(F32) * (1.0 / (2 * FAC))
    place = iota((cells, 384), 0)
    first = jnp.clip(point, 0, cells - 1)
    second = jnp.clip(point + 1, 0, cells - 1)
    spread[...] = (
        jnp.where(place == first, 1.0 - fraction, 0.0) + jnp.where(place == second, fraction, 0.0)
    ).astype(BF16)

    def many(count, sem, half):
        return pltpu.make_async_remote_copy(
            src_ref=rows_in.at[half, pl.ds(0, count)],
            dst_ref=rows_in.at[half, pl.ds(0, count)],
            send_sem=fsend.at[2 * sem + half],
            recv_sem=frecv.at[2 * sem + half],
            device_id=(r, c),
            device_id_type=MESH,
        )

    for half, needed in ((0, low_half), (1, high_half)):

        @pl.when(needed)
        def _():
            many(n_col - 1, 0, half).wait_recv()

            @pl.when(has_up)
            def _():
                many(1, 1, half).wait_recv()

            @pl.when(has_down)
            def _():
                many(1, 2, half).wait_recv()

            @pl.when(jnp.logical_not(has_up))
            def _():
                rows_in[half, 0] = rows_in[half, 1]

            @pl.when(jnp.logical_not(has_down))
            def _():
                rows_in[half, n_col + 1] = rows_in[half, n_col]

    points = jnp.concatenate(
        [rows_in[half].reshape((n_col + 2) * 8, cells // 2) for half in range(2)], axis=1
    )
    high, rest = split(points)
    middle, low = split(points - high.astype(F32))
    weights = spread[...]
    wide = nn(high, weights) + (nn(middle, weights) + nn(low, weights))
    var = jnp.bitwise_and(iota((wide.shape[0], 128), 0), 7)
    scale, shift = jnp.zeros(var.shape, F32), jnp.zeros(var.shape, F32)
    for v, (slope, start) in enumerate(
        (
            (20.0, -10.0 + 6.5 * 0.5),
            (0.8 * MELT, 0.0),
            (0.15 * MELT, (0.25 - 0.3) * MELT),
            (0.2 * 1.5, 0.0),
            (6.0, 0.5),
            (4.0, 0.0),
        )
    ):
        scale = jnp.where(var == v, slope, scale)
        shift = jnp.where(var == v, start, shift)
    for t in range(3):
        part = wide[:, 128 * t : 128 * t + 128]
        height = pltpu.roll(part, part.shape[0] - 6, 0)
        part = part * scale + shift + jnp.where(var == 0, 13.0 * height, 0.0)
        coarse[0, t] = part
        coarse[1, t, 0 : (n_col + 1) * 8, :] = part[8:] - part[:-8]

    @pl.when(has_up)
    def _():
        for copy in row_copies(1, r - 1):
            copy.wait_recv()
        for copy in row_copies(0, r - 1):
            copy.wait_send()
        for t in range(2):
            for d in range(8):
                ext[WEIGHT + d, t, pl.ds(TOP - RIM, RIM), :] = wrim[
                    1, d, :, pl.ds(128 * t, 128)
                ].astype(F32)

    @pl.when(has_down)
    def _():
        for copy in row_copies(0, r + 1):
            copy.wait_recv()
        for copy in row_copies(1, r + 1):
            copy.wait_send()
        for t in range(2):
            for d in range(8):
                ext[WEIGHT + d, t, pl.ds(TOP + TILE, RIM), :] = wrim[
                    0, d, :, pl.ds(128 * t, 128)
                ].astype(F32)

    for out in (first_out, second_out):
        out[:, 0 : TOP - RIM, :] = jnp.zeros((3, TOP - RIM, 128), F32)
        out[:, TOP + TILE + RIM :, :] = jnp.zeros((3, RIM, 128), F32)

    def balance(k, t):
        rows = pl.ds(pl.multiple_of(TOP - RIM + FAC * k, 8), FAC)
        part = (2 * iota((FAC, 128), 0) + 1).astype(F32) * (1.0 / (2 * FAC))
        v = []
        for var in range(6):
            at = pl.ds(k * 8 + var, 1)
            v.append(coarse[0, t, at, :] + coarse[1, t, at, :] * part)
        heat, solar, thermal, deficit, breeze, rain = v
        heat = heat - 6.5 * ext[GROUND, t, rows, :]
        frozen = rain / (1.0 + jnp.exp(heat * (1.0 / 1.5)))
        liquid = rain - frozen
        budget = (solar - solar * ext[REFLECTED, t, rows, :]) + thermal
        budget = budget + (0.02 * MELT) * breeze * heat
        pack = ext[SNOW, t, rows, :] + frozen
        melted = jnp.minimum(jnp.maximum(budget, 0.0), pack)
        wetted = ext[SOIL, t, rows, :] + liquid + melted
        demand = (0.3 / MELT) * solar + (deficit + (0.1 * deficit) * breeze)
        evaporation = demand * wetted / (wetted + 2.0)
        remaining = wetted - evaporation
        recharge = 0.4 * jnp.maximum(remaining - 6.0, 0.0)
        storage = ext[STORE, t, rows, :] + recharge
        ext[STORE, t, rows, :] = storage
        first_out[t, rows, :] = ext[RATE, t, rows, :] * storage
        if t < 2:
            snow_out[t, rows, :] = pack - melted
            soil_out[t, rows, :] = remaining - recharge
            drained[t, rows, :] = jnp.zeros((FAC, 128), F32)

    balance(0, 0)
    balance(0, 1)

    @pl.loop(0, TILE // FAC // 2)
    def _(i):
        for k in range(2):
            for t in range(2):
                balance(2 * i + 1 + k, t)

    each_strip(lambda copy: copy.wait_recv(), False)

    def unpack(source, target, rows, right_ok, left_ok):
        lane = iota((rows, 128), 1)
        kept = jnp.logical_or(
            jnp.logical_and(lane < RIM, right_ok), jnp.logical_and(lane >= 128 - RIM, left_ok)
        )
        from_right = rims[0, source, :]
        from_left = pltpu.roll(rims[1, source, :], 128 - 8, 1)
        first_half = jnp.bitwise_and(lane, 15) < 8
        pairs = (
            jnp.where(first_half, from_right, from_left),
            jnp.where(first_half, from_left, from_right),
        )
        for k in range(ARRAYS):
            x = pairs[k % 2]
            x = pltpu.roll(x, 128 - 8 * k, 1) if k else x
            ext[k, 2, target, :] = jnp.where(kept, x, 0.0)

    @pl.loop(0, TILE // step_rows)
    def _(i):
        unpack(
            pl.ds(pl.multiple_of(RIM + i * step_rows, 8), step_rows),
            pl.ds(pl.multiple_of(TOP + i * step_rows, 8), step_rows),
            step_rows,
            has_right,
            has_left,
        )

    for source, ok in ((0, has_up), (RIM + TILE, has_down)):
        unpack(
            pl.ds(source, RIM),
            pl.ds(TOP - RIM + source, RIM),
            RIM,
            jnp.logical_and(has_right, ok),
            jnp.logical_and(has_left, ok),
        )

    balance(0, 2)

    @pl.loop(0, TILE // FAC // 4)
    def _(i):
        for k in range(4):
            balance(4 * i + 1 + k, 2)

    def sweep(now, later):
        for q in range((TILE + 2 * RIM) // 16):
            base = TOP - RIM + 16 * q
            rows = pl.ds(base, 16)
            lane = iota((16, 128), 1)
            sums = {-1: [], 0: [], 1: []}
            middle = []
            for t in range(3):
                parts = {-1: None, 0: None, 1: None}
                for down_row in (-1, 0, 1):
                    at = pl.ds(base - down_row, 16)
                    out = now[t, at, :]
                    if down_row == 0:
                        middle.append(out)
                    for direction, (dr, dc) in enumerate(OFFSETS):
                        if dr == down_row:
                            term = ext[WEIGHT + direction, t, at, :] * out
                            parts[dc] = term if parts[dc] is None else parts[dc] + term
                for dc in (-1, 0, 1):
                    sums[dc].append(parts[dc])
            east = [pltpu.roll(x, 1, 1) for x in sums[1]]
            west = [pltpu.roll(x, 127, 1) for x in sums[-1]]
            for t in range(3):
                inflow = (
                    sums[0][t]
                    + jnp.where(lane == 0, east[(t + 2) % 3], east[t])
                    + jnp.where(lane == 127, west[(t + 1) % 3], west[t])
                )
                storage = (ext[STORE, t, rows, :] - middle[t]) + inflow
                ext[STORE, t, rows, :] = storage
                later[t, rows, :] = ext[RATE, t, rows, :] * storage
                if t < 2:
                    drained[t, rows, :] = drained[t, rows, :] + middle[t]

    @pl.loop(0, SWEEPS // 2)
    def _(i):
        @pl.when(i == 1)
        def _():
            @pl.loop(1, SIDE)
            def _(k):
                slot = lax.rem(across + k, SIDE)
                matrix_copy(slot, slot).wait_recv()

            after[1] = mats[SIDE - 1]
            tmat[1] = mats[jnp.where(across > 0, across - 1, SIDE)]

        after[i + 1] = product(after[i], mats[jnp.where(i > 0, SIDE - 1 - i, SIDE)])
        started = jnp.logical_and(i > 0, i < across)
        tmat[i + 1] = product(tmat[i], mats[jnp.where(started, across - 1 - i, SIDE)])
        sweep(first_out, second_out)
        sweep(second_out, first_out)

    def group_copy(to, slot):
        return pltpu.make_async_remote_copy(
            src_ref=after.at[SIDE],
            dst_ref=gmats.at[slot],
            send_sem=qsend.at[to],
            recv_sem=qrecv.at[slot],
            device_id=(r, to * SIDE + across),
            device_id_type=MESH,
        )

    @pl.loop(group + 1, n_col // SIDE)
    def _(later):
        group_copy(later, group).start()

    for t in range(2):
        own = pl.ds(TOP, TILE)
        ground_out[t, own, :] = ext[STORE, t, own, :]
        drained[t, own, :] = drained[t, own, :] * retained[t, own, :]

    def build(piece):
        top = iota((8, 128), 0)
        for b in range(NBLK):
            for i in range(4 * piece, 4 * piece + 4):
                for t in range(2):
                    lanes = pl.ds(TILE * i + 128 * t, 128)
                    row = b * BR + i
                    same = lax.shift_right_logical(seg[t, row : row + 1, :], 4) == top
                    kept = jnp.where(same, drained[t, TOP + row : TOP + row + 1, :], 0.0)
                    high, low = split(kept)
                    ahot[16 * b : 16 * b + 8, lanes] = high
                    ahot[16 * b + 8 : 16 * b + 16, lanes] = low

    build(0)
    for i in range(4):
        if i < 3:
            build(i + 1)
        wide = pl.ds(4 * TILE * i, 4 * TILE)
        piece = nt(ahot[:, wide], bhot[:, wide])
        for t in range(2):
            half = piece[:, 128 * t : 128 * t + 128]
            hot[t] = half if i == 0 else hot[t] + half

    lane = iota((8, 128), 1)
    sixteen = lax.shift_right_logical(lane, 4)
    for b in range(NBLK):
        t = b // 8
        x = hot[t, b * 16 : b * 16 + 8, :] + hot[t, b * 16 + 8 : b * 16 + 16, :]
        x = jnp.where(sixteen == b % 8, x, 0.0)
        for shift in (16, 32, 64):
            x = x + pltpu.roll(x, shift, 1)
        x = jnp.where(sixteen == iota((8, 128), 0), x, 0.0)
        lat[b : b + 1, :] = 0.001 * jnp.sum(x, axis=0, keepdims=True)

    def to_row(matrix):
        column = jnp.sum(matrix, axis=1, keepdims=True)
        same = iota((SEG, SEG), 0) == iota((SEG, SEG), 1)
        return jnp.sum(jnp.where(same, column, 0.0), axis=0, keepdims=True)

    total = wmat[0] * lat[0:1, :]
    for b in range(1, NBLK):
        total = total + wmat[b] * lat[b : b + 1, :]
    leaving = to_row(total)
    gsend[0:1, :] = leaving
    gsend[1:2, :] = to_row(after[SIDE - 1 - across] * leaving)

    def leaving_copy(col, slot):
        return pltpu.make_async_remote_copy(
            src_ref=gsend,
            dst_ref=gin.at[slot],
            send_sem=gsend_sem.at[col],
            recv_sem=grecv.at[slot],
            device_id=(r, col),
            device_id_type=MESH,
        )

    @pl.loop(c + 1, n_col)
    def _(col):
        leaving_copy(col, c).start()

    @pl.loop(0, NBLK)
    def _(b):
        source = lat[pl.ds(b, 1), :]
        carried = jnp.zeros((SEG, SEG), F32)
        for back in range(1, 4):
            share = trans[pl.ds(b + 3 - back, 1), :] * drains_here(b, back)
            carried = carried + fmat[b + 3 - back] * share
            source = source + share * flow0[pl.ds(b + 3 - back, 1), :]
        fmat[b + 3] = product_nt(carried, inv[b])
        flow0[pl.ds(b + 3, 1), :] = to_row(inv[b] * source)

    @pl.loop(0, group)
    def _(slot):
        group_copy(group, slot).wait_recv()

    reach = [tmat[across]]
    for j in range(n_col // SIDE - 2):
        slot = jnp.where(j < group, group - 1 - j, n_col // SIDE)
        reach.append(product(reach[j], gmats[slot]))

    @pl.loop(0, c)
    def _(slot):
        leaving_copy(c, slot).wait_recv()

    total = jnp.zeros((SEG, SEG), F32)
    for j in range(n_col // SIDE - 1):
        arriving = jnp.zeros((1, SEG), F32)
        for k in range(SIDE):
            slot = jnp.where(j < group, (group - 1 - j) * SIDE + k, c)
            arriving = arriving + gin[slot, 1:2, :]
        total = total + reach[j] * arriving
    for k in range(SIDE - 1):
        slot = jnp.where(k < across, c - 1 - k, c)
        total = total + tmat[k] * gin[slot, 0:1, :]
    entering = jnp.sum(total, axis=1, keepdims=True)

    for b in range(NBLK):
        extra = jnp.sum(fmat[b + 3] * entering, axis=0, keepdims=True)
        flow_out[b : b + 1, :] = flow0[b + 3 : b + 4, :] + extra

    for half, needed in ((0, low_half), (1, high_half)):

        @pl.when(needed)
        def _():
            many(n_col // 2, 0, half).wait_send()

        @pl.when(jnp.logical_not(needed))
        def _():
            many(n_col // 2 + 1, 0, half).wait_send()

        for sem, sends in ((1, sends_down), (2, sends_up)):

            @pl.when(sends)
            def _():
                many(n_col // 2 + 1, sem, half).wait_send()

    @pl.loop(1, SIDE)
    def _(k):
        matrix_copy(lax.rem(across + k, SIDE), across).wait_send()

    @pl.loop(group + 1, n_col // SIDE)
    def _(later):
        group_copy(later, group).wait_send()

    each_strip(lambda copy: copy.wait_send(), True)

    @pl.loop(c + 1, n_col)
    def _(col):
        leaving_copy(col, c).wait_send()


def writer(*refs):
    snow, soil, water, flow, snow_out, soil_out, ground_out, flow_out, sems = refs
    copies = [pltpu.make_async_copy(flow, flow_out, sems.at[6])]
    for k, (ref, out) in enumerate(((snow, snow_out), (soil, soil_out), (water, ground_out))):
        for t in range(2):
            copies.append(
                pltpu.make_async_copy(
                    ref.at[t, pl.ds(TOP, TILE), :],
                    out.at[:, pl.ds(128 * t, 128)],
                    sems.at[2 * k + t],
                )
            )
    for copy in copies:
        copy.start()
    for copy in copies:
        copy.wait()


def per_device(n_row, n_col, forcing, *args):
    *args, downstream = args
    cells = forcing.shape[2]
    any_space = pl.BlockSpec(memory_space=pl.ANY)
    vmem = pl.BlockSpec(memory_space=pltpu.VMEM)
    smem = pl.BlockSpec(memory_space=pltpu.SMEM)
    tile = jax.ShapeDtypeStruct((TILE, TILE), F32)
    flows = jax.ShapeDtypeStruct((NBLK, SEG), F32)
    dma = pltpu.SemaphoreType.DMA
    results = pl.pallas_call(
        functools.partial(kernel, n_row, n_col),
        out_shape=(*(pltpu.VMEM((2, ROWS, 128), F32) for _ in range(3)), pltpu.VMEM((NBLK, SEG), F32)),
        in_specs=[vmem] + [any_space] * 9 + [vmem, smem],
        out_specs=(vmem, vmem, vmem, vmem),
        scratch_shapes=[
            pltpu.VMEM((ARRAYS, 3, ROWS, 128), F32),
            pltpu.VMEM((8, TILE, TILE), BF16),
            pltpu.VMEM((2, TILE, 128), jnp.int32),
            pltpu.VMEM((NBLK, SEG, SEG), F32),
            pltpu.VMEM((NBLK + 1, SEG, SEG), F32),
            pltpu.VMEM((NBLK + 3, SEG, SEG), F32),
            pltpu.VMEM((SIDE + 1, SEG, SEG), F32),
            pltpu.VMEM((SIDE + 1, SEG, SEG), F32),
            pltpu.VMEM((SIDE + 1, SEG, SEG), F32),
            pltpu.VMEM((n_col // SIDE + 1, SEG, SEG), F32),
            pltpu.VMEM((TILE, BR * TILE), BF16),
            pltpu.VMEM((TILE, BR * TILE), BF16),
            pltpu.VMEM((2, TILE, 128), F32),
            pltpu.VMEM((2, TILE, 128), F32),
            pltpu.VMEM((2, TILE + 2 * RIM, 128), F32),
            pltpu.VMEM((2, 8, RIM, TILE), BF16),
            pltpu.VMEM((2, 8, cells // 2), F32),
            pltpu.VMEM((2, n_col + 2, 8, cells // 2), F32),
            pltpu.VMEM((cells, 384), BF16),
            pltpu.VMEM((2, 3, (n_col + 2) * 8, 128), F32),
            pltpu.VMEM((3, ROWS, 128), F32),
            pltpu.VMEM((3, ROWS, 128), F32),
            pltpu.VMEM((2, ROWS, 128), F32),
            pltpu.VMEM((2, ROWS, 128), F32),
            pltpu.VMEM((24, SEG), F32),
            pltpu.VMEM((NBLK, SEG), F32),
            pltpu.VMEM((24, SEG), F32),
            pltpu.VMEM((8, SEG), F32),
            pltpu.VMEM((n_col, 8, SEG), F32),
            dma((4,)),
            dma((6,)),
            dma((6,)),
            dma((6,)),
            dma((6,)),
            dma((4,)),
            dma((4,)),
            dma((SIDE,)),
            dma((SIDE,)),
            dma((n_col // SIDE,)),
            dma((n_col // SIDE,)),
            dma((n_col,)),
            dma((n_col,)),
        ],
        compiler_params=pltpu.CompilerParams(
            collective_id=0, has_side_effects=True
        ),
        name="hydrology",
    )(forcing, *args, downstream.T)
    return pl.pallas_call(
        writer,
        out_shape=(tile, tile, tile, flows),
        in_specs=[any_space] * 4,
        out_specs=(any_space,) * 4,
        scratch_shapes=[dma((7,))],
        compiler_params=pltpu.CompilerParams(vmem_limit_bytes=1 << 20),
        name="writer",
    )(*results)


def solution(mesh):
    n_row, n_col = mesh.shape["row"], mesh.shape["col"]
    tiles = P("row", "col")
    placed = (
        P(None, ("row", "col"), None),
        *(tiles for _ in range(6)),
        P(None, "row", "col"),
        tiles,
        P("row", "col", None),
        tiles,
        tiles,
    )
    return jax.shard_map(
        functools.partial(per_device, n_row, n_col),
        mesh=mesh,
        in_specs=placed,
        out_specs=(tiles, tiles, tiles, tiles),
        check_vma=False,
    )
```

```python
import functools

import jax
import jax.numpy as jnp
from jax import lax
from jax.experimental import pallas as pl
from jax.experimental.pallas import tpu as pltpu
from jax.sharding import PartitionSpec as P

MESH = pl.DeviceIdType.MESH
F32, BF16 = jnp.float32, jnp.bfloat16

FAC = 16
VARS = 7
SEG = 128
SWEEPS = 8
NBLK = 16
BR = 16
TILE = 256
RIM = 8
TOP = 16
ROWS = TILE + 32
OFFSETS = ((-1, -1), (-1, 0), (-1, 1), (0, -1), (0, 1), (1, -1), (1, 0), (1, 1))
GROUND, REFLECTED, SNOW, SOIL, STORE, RATE, WEIGHT = range(7)
ARRAYS = 14
MELT = 10.8
SIDE = 4


def split(x):
    high = x.astype(BF16)
    return high, (x - high.astype(F32)).astype(BF16)


def nn(a, b):
    return lax.dot_general(a, b, (((1,), (0,)), ((), ())), preferred_element_type=F32)


def nt(a, b):
    return lax.dot_general(a, b, (((1,), (1,)), ((), ())), preferred_element_type=F32)


def both(x, axis):
    return jnp.concatenate(split(x), axis=axis)


def product(a, b):
    right = both(b, 1)
    wide = nn(both(a, 1), jnp.concatenate([right, right], axis=0))
    return wide[:, :SEG] + wide[:, SEG:]


def product_nt(a, b):
    right = both(b, 0)
    wide = nt(both(a, 1), jnp.concatenate([right, right], axis=1))
    return wide[:, :SEG] + wide[:, SEG:]


def iota(shape, dim):
    return lax.broadcasted_iota(jnp.int32, shape, dim)


def kernel(
    n_row,
    n_col,
    forcing,
    ground,
    reflected,
    snow_water,
    soil_water,
    saturated,
    release,
    mfd,
    segment,
    route,
    transfer,
    downstream,
    snow_out,
    soil_out,
    ground_out,
    flow_out,
    ext,
    wb,
    seg,
    inv,
    wmat,
    fmat,
    mats,
    after,
    tmat,
    gmats,
    ahot,
    bhot,
    hot,
    strips,
    rims,
    wrim,
    mine,
    rows_in,
    spread,
    coarse,
    first_out,
    second_out,
    drained,
    retained,
    trans,
    lat,
    flow0,
    gsend,
    gin,
    load_sem,
    fsend,
    frecv,
    ssend,
    srecv,
    rsend,
    rrecv,
    msend,
    mrecv,
    qsend,
    qrecv,
    gsend_sem,
    grecv,
):
    r, c = lax.axis_index("row"), lax.axis_index("col")
    has_up, has_down = r > 0, r < n_row - 1
    has_left, has_right = c > 0, c < n_col - 1

    barrier = pltpu.get_barrier_semaphore()

    def greet(row, col):
        pl.semaphore_signal(barrier, inc=1, device_id=(row, col), device_id_type=MESH)

    for d in range(1, n_col):
        greet(r, lax.rem(c + d, n_col))

    @pl.when(has_up)
    def _():
        greet(r - 1, c)
        greet(r - 1, n_col - 1)

        @pl.when(has_left)
        def _():
            greet(r - 1, c - 1)

        @pl.when(has_right)
        def _():
            greet(r - 1, c + 1)

    @pl.when(has_down)
    def _():
        greet(r + 1, c)
        greet(r + 1, 0)

        @pl.when(has_left)
        def _():
            greet(r + 1, c - 1)

        @pl.when(has_right)
        def _():
            greet(r + 1, c + 1)

    for k, ref in enumerate((ground, reflected, snow_water, soil_water, saturated, release)):
        for t in range(2):
            pltpu.make_async_copy(
                ref.at[:, pl.ds(128 * t, 128)], ext.at[k, t, pl.ds(TOP, TILE), :], load_sem.at[0]
            ).start()
    load_weights = pltpu.make_async_copy(mfd, wb, load_sem.at[1])
    load_weights.start()
    load_route = pltpu.make_async_copy(route, inv, load_sem.at[2])
    load_route.start()
    for t in range(2):
        pltpu.make_async_copy(
            segment.at[:, pl.ds(128 * t, 128)], seg.at[t], load_sem.at[3]
        ).start()

    eye = (iota((SEG, SEG), 0) == iota((SEG, SEG), 1)).astype(F32)
    wmat[NBLK] = eye
    after[0] = eye
    tmat[0] = eye
    mats[SIDE] = jnp.zeros((SEG, SEG), F32)
    gmats[n_col // SIDE] = jnp.zeros((SEG, SEG), F32)
    gin[c] = jnp.zeros((8, SEG), F32)
    gsend[...] = jnp.zeros((8, SEG), F32)
    fmat[0] = jnp.zeros((SEG, SEG), F32)
    fmat[1] = jnp.zeros((SEG, SEG), F32)
    fmat[2] = eye
    trans[0:3, :] = jnp.ones((3, SEG), F32)
    trans[3 : 3 + NBLK, :] = transfer[...]
    flow0[0:3, :] = jnp.zeros((3, SEG), F32)
    low_half, high_half = c <= n_col // 2, c >= n_col // 2 - 1
    for half in range(2):
        lanes = pl.ds(half * mine.shape[2], mine.shape[2])
        for v in range(VARS):
            mine[half, v : v + 1, :] = forcing[v, :, lanes]
        mine[half, VARS : VARS + 1, :] = jnp.zeros((1, mine.shape[2]), F32)

    @pl.when(jnp.logical_not(low_half))
    def _():
        rows_in[0] = jnp.zeros(rows_in.shape[1:], F32)

    @pl.when(jnp.logical_not(high_half))
    def _():
        rows_in[1] = jnp.zeros(rows_in.shape[1:], F32)

    @pl.when(low_half)
    def _():
        rows_in[0, c + 1] = mine[0]

    @pl.when(high_half)
    def _():
        rows_in[1, c + 1] = mine[1]

    @pl.when(jnp.logical_not(has_up))
    def _():
        ext[:, :, pl.ds(TOP - RIM, RIM), :] = jnp.zeros((ARRAYS, 3, RIM, 128), F32)

    @pl.when(jnp.logical_not(has_down))
    def _():
        ext[:, :, pl.ds(TOP + TILE, RIM), :] = jnp.zeros((ARRAYS, 3, RIM, 128), F32)

    load_weights.wait()
    six = ext.at[pl.ds(0, WEIGHT), pl.ds(0, 2), pl.ds(TOP, TILE), :]
    pltpu.make_async_copy(six, six, load_sem.at[0]).wait()

    step_rows = 64

    def pack_side(side):
        @pl.loop(0, TILE // step_rows)
        def _(i):
            here = pl.ds(pl.multiple_of(i * step_rows, step_rows), step_rows)
            there = pl.ds(pl.multiple_of(TOP + i * step_rows, 8), step_rows)
            lane = iota((step_rows, 128), 1)
            packed = jnp.zeros((step_rows, 128), F32)
            for k in range(ARRAYS):
                if k < WEIGHT:
                    x = ext[k, side, there, :]
                else:
                    x = wb[k - WEIGHT, here, pl.ds(128 * side, 128)].astype(F32)
                shift = (8 * k + 8 * side) % 128
                place = jnp.logical_and(lane >= 8 * k, lane < 8 * k + 8)
                packed = jnp.where(place, pltpu.roll(x, shift, 1) if shift else x, packed)
            strips[side, here, :] = packed

    pack_side(1)
    pack_side(0)

    def strip_copies(side, row_step, row, col):
        source, target, rows = {
            0: (0, RIM, TILE),
            -1: (0, RIM + TILE, RIM),
            1: (TILE - RIM, 0, RIM),
        }[row_step]
        return pltpu.make_async_remote_copy(
            src_ref=strips.at[side, pl.ds(source, rows), :],
            dst_ref=rims.at[side, pl.ds(target, rows), :],
            send_sem=ssend.at[3 * side + row_step + 1],
            recv_sem=srecv.at[3 * side + row_step + 1],
            device_id=(row, col),
            device_id_type=MESH,
        )

    def each_strip(act, sending, sides=(0, 1)):
        for side in sides:
            toward_left = (side == 0) == sending
            there, col = (has_left, c - 1) if toward_left else (has_right, c + 1)
            for row_step in (0, -1, 1):
                ok, row = there, r
                if row_step:
                    toward_up = (row_step == -1) == sending
                    ok = jnp.logical_and(there, has_up if toward_up else has_down)
                    row = r - 1 if toward_up else r + 1

                @pl.when(ok)
                def _():
                    act(strip_copies(side, row_step, row, col))

    pl.semaphore_wait(
        barrier,
        n_col
        - 1
        + (has_up.astype(jnp.int32) + has_down.astype(jnp.int32))
        * (1 + has_left.astype(jnp.int32) + has_right.astype(jnp.int32))
        + jnp.where(jnp.logical_and(c == n_col - 1, has_down), n_col, 0)
        + jnp.where(jnp.logical_and(c == 0, has_up), n_col, 0),
    )

    def forcing_copy(half, row, col, slot, sem):
        return pltpu.make_async_remote_copy(
            src_ref=mine.at[half],
            dst_ref=rows_in.at[half, slot],
            send_sem=fsend.at[2 * sem + half],
            recv_sem=frecv.at[2 * sem + half],
            device_id=(row, col),
            device_id_type=MESH,
        )

    halves = ((0, 0, n_col // 2 + 1), (1, n_col // 2 - 1, n_col))
    sends_down = jnp.logical_and(c == n_col - 1, has_down)
    sends_up = jnp.logical_and(c == 0, has_up)

    @pl.when(sends_down)
    def _():
        for half, start, stop in halves:

            @pl.loop(start, stop)
            def _(d):
                forcing_copy(half, r + 1, d, 0, 1).start()

    @pl.when(sends_up)
    def _():
        for half, start, stop in halves:

            @pl.loop(start, stop)
            def _(d):
                forcing_copy(half, r - 1, d, n_col + 1, 2).start()

    for half, start, stop in halves:

        @pl.loop(start, stop)
        def _(d):
            @pl.when(d != c)
            def _():
                forcing_copy(half, r, d, c + 1, 0).start()

    each_strip(lambda copy: copy.start(), True, (1,))

    def row_copies(side, row):
        source, target = (0, TOP + TILE) if side == 0 else (TILE - RIM, TOP - RIM)

        def remote(src, dst, n):
            return pltpu.make_async_remote_copy(
                src_ref=src,
                dst_ref=dst,
                send_sem=rsend.at[2 * side + n],
                recv_sem=rrecv.at[2 * side + n],
                device_id=(row, c),
                device_id_type=MESH,
            )

        inputs = pl.ds(0, WEIGHT)
        two = pl.ds(0, 2)
        return (
            remote(
                ext.at[inputs, two, pl.ds(TOP + source, RIM), :],
                ext.at[inputs, two, pl.ds(target, RIM), :],
                0,
            ),
            remote(wb.at[:, pl.ds(source, RIM), :], wrim.at[side], 1),
        )

    @pl.when(has_up)
    def _():
        for copy in row_copies(0, r - 1):
            copy.start()

    @pl.when(has_down)
    def _():
        for copy in row_copies(1, r + 1):
            copy.start()

    each_strip(lambda copy: copy.start(), True, (0,))

    load_route.wait()
    pltpu.make_async_copy(seg, seg, load_sem.at[3]).wait()

    def drains_here(block, back):
        before = block - back
        drains = downstream[0, jnp.maximum(before, 0)] == block
        first = jnp.logical_and(block == 0, back == 1)
        return jnp.where(before >= 0, drains, first).astype(F32)

    @pl.loop(0, NBLK)
    def _(i):
        b = NBLK - 1 - i
        later = wmat[downstream[0, b]] * trans[pl.ds(b + 3, 1), :]
        wmat[b] = product(later, inv[b])

        target = pl.ds(pl.multiple_of(i * 16, 16), 16)
        low_part = iota((16, 128), 0)
        for j in range(BR):
            for t in range(2):
                same = jnp.bitwise_and(seg[t, pl.ds(i * BR + j, 1), :], 15) == low_part
                bhot[target, pl.ds(j * TILE + 128 * t, 128)] = jnp.where(same, 1.0, 0.0).astype(
                    BF16
                )

        there = pl.ds(pl.multiple_of(TOP + i * 16, 8), 16)
        for t in range(2):
            kept = None
            for d in range(8):
                x = wb[d, target, pl.ds(128 * t, 128)].astype(F32)
                ext[WEIGHT + d, t, there, :] = x
                kept = x if kept is None else kept + x
            retained[t, there, :] = 1.0 - kept

    across, group = lax.rem(c, SIDE), lax.div(c, SIDE)

    def matrix_copy(to, slot):
        return pltpu.make_async_remote_copy(
            src_ref=wmat.at[0],
            dst_ref=mats.at[slot],
            send_sem=msend.at[to],
            recv_sem=mrecv.at[slot],
            device_id=(r, group * SIDE + to),
            device_id_type=MESH,
        )

    @pl.loop(1, SIDE)
    def _(k):
        matrix_copy(lax.rem(across + k, SIDE), across).start()

    mats[across] = wmat[0]

    cells = 2 * rows_in.shape[3]
    lanes = iota((cells, 384), 1)
    column = jnp.where(lanes < 320, lanes, lanes - 384) + c * TILE
    numerator = 2 * column + 1 - FAC
    point = lax.shift_right_arithmetic(numerator, 5)
    fraction = (numerator - 2 * FAC * point).astype(F32) * (1.0 / (2 * FAC))
    place = iota((cells, 384), 0)
    first = jnp.clip(point, 0, cells - 1)
    second = jnp.clip(point + 1, 0, cells - 1)
    spread[...] = (
        jnp.where(place == first, 1.0 - fraction, 0.0) + jnp.where(place == second, fraction, 0.0)
    ).astype(BF16)

    def many(count, sem, half):
        return pltpu.make_async_remote_copy(
            src_ref=rows_in.at[half, pl.ds(0, count)],
            dst_ref=rows_in.at[half, pl.ds(0, count)],
            send_sem=fsend.at[2 * sem + half],
            recv_sem=frecv.at[2 * sem + half],
            device_id=(r, c),
            device_id_type=MESH,
        )

    for half, needed in ((0, low_half), (1, high_half)):

        @pl.when(needed)
        def _():
            many(n_col - 1, 0, half).wait_recv()

            @pl.when(has_up)
            def _():
                many(1, 1, half).wait_recv()

            @pl.when(has_down)
            def _():
                many(1, 2, half).wait_recv()

            @pl.when(jnp.logical_not(has_up))
            def _():
                rows_in[half, 0] = rows_in[half, 1]

            @pl.when(jnp.logical_not(has_down))
            def _():
                rows_in[half, n_col + 1] = rows_in[half, n_col]

    points = jnp.concatenate(
        [rows_in[half].reshape((n_col + 2) * 8, cells // 2) for half in range(2)], axis=1
    )
    high, rest = split(points)
    middle, low = split(points - high.astype(F32))
    weights = spread[...]
    wide = nn(high, weights) + (nn(middle, weights) + nn(low, weights))
    var = jnp.bitwise_and(iota((wide.shape[0], 128), 0), 7)
    scale, shift = jnp.zeros(var.shape, F32), jnp.zeros(var.shape, F32)
    for v, (slope, start) in enumerate(
        (
            (20.0, -10.0 + 6.5 * 0.5),
            (0.8 * MELT, 0.0),
            (0.15 * MELT, (0.25 - 0.3) * MELT),
            (0.2 * 1.5, 0.0),
            (6.0, 0.5),
            (4.0, 0.0),
        )
    ):
        scale = jnp.where(var == v, slope, scale)
        shift = jnp.where(var == v, start, shift)
    for t in range(3):
        part = wide[:, 128 * t : 128 * t + 128]
        height = pltpu.roll(part, part.shape[0] - 6, 0)
        part = part * scale + shift + jnp.where(var == 0, 13.0 * height, 0.0)
        coarse[0, t] = part
        coarse[1, t, 0 : (n_col + 1) * 8, :] = part[8:] - part[:-8]

    @pl.when(has_up)
    def _():
        for copy in row_copies(1, r - 1):
            copy.wait_recv()
        for copy in row_copies(0, r - 1):
            copy.wait_send()
        for t in range(2):
            for d in range(8):
                ext[WEIGHT + d, t, pl.ds(TOP - RIM, RIM), :] = wrim[
                    1, d, :, pl.ds(128 * t, 128)
                ].astype(F32)

    @pl.when(has_down)
    def _():
        for copy in row_copies(0, r + 1):
            copy.wait_recv()
        for copy in row_copies(1, r + 1):
            copy.wait_send()
        for t in range(2):
            for d in range(8):
                ext[WEIGHT + d, t, pl.ds(TOP + TILE, RIM), :] = wrim[
                    0, d, :, pl.ds(128 * t, 128)
                ].astype(F32)

    for out in (first_out, second_out):
        out[:, 0 : TOP - RIM, :] = jnp.zeros((3, TOP - RIM, 128), F32)
        out[:, TOP + TILE + RIM :, :] = jnp.zeros((3, RIM, 128), F32)

    def balance(k, t):
        rows = pl.ds(pl.multiple_of(TOP - RIM + FAC * k, 8), FAC)
        part = (2 * iota((FAC, 128), 0) + 1).astype(F32) * (1.0 / (2 * FAC))
        v = []
        for var in range(6):
            at = pl.ds(k * 8 + var, 1)
            v.append(coarse[0, t, at, :] + coarse[1, t, at, :] * part)
        heat, solar, thermal, deficit, breeze, rain = v
        heat = heat - 6.5 * ext[GROUND, t, rows, :]
        frozen = rain / (1.0 + jnp.exp(heat * (1.0 / 1.5)))
        liquid = rain - frozen
        budget = (solar - solar * ext[REFLECTED, t, rows, :]) + thermal
        budget = budget + (0.02 * MELT) * breeze * heat
        pack = ext[SNOW, t, rows, :] + frozen
        melted = jnp.minimum(jnp.maximum(budget, 0.0), pack)
        wetted = ext[SOIL, t, rows, :] + liquid + melted
        demand = (0.3 / MELT) * solar + (deficit + (0.1 * deficit) * breeze)
        evaporation = demand * wetted / (wetted + 2.0)
        remaining = wetted - evaporation
        recharge = 0.4 * jnp.maximum(remaining - 6.0, 0.0)
        storage = ext[STORE, t, rows, :] + recharge
        ext[STORE, t, rows, :] = storage
        first_out[t, rows, :] = ext[RATE, t, rows, :] * storage
        if t < 2:
            snow_out[t, rows, :] = pack - melted
            soil_out[t, rows, :] = remaining - recharge
            drained[t, rows, :] = jnp.zeros((FAC, 128), F32)

    balance(0, 0)
    balance(0, 1)

    @pl.loop(0, TILE // FAC // 2)
    def _(i):
        for k in range(2):
            for t in range(2):
                balance(2 * i + 1 + k, t)

    each_strip(lambda copy: copy.wait_recv(), False)

    def unpack(source, target, rows, right_ok, left_ok):
        lane = iota((rows, 128), 1)
        kept = jnp.logical_or(
            jnp.logical_and(lane < RIM, right_ok), jnp.logical_and(lane >= 128 - RIM, left_ok)
        )
        from_right = rims[0, source, :]
        from_left = pltpu.roll(rims[1, source, :], 128 - 8, 1)
        first_half = jnp.bitwise_and(lane, 15) < 8
        pairs = (
            jnp.where(first_half, from_right, from_left),
            jnp.where(first_half, from_left, from_right),
        )
        for k in range(ARRAYS):
            x = pairs[k % 2]
            x = pltpu.roll(x, 128 - 8 * k, 1) if k else x
            ext[k, 2, target, :] = jnp.where(kept, x, 0.0)

    @pl.loop(0, TILE // step_rows)
    def _(i):
        unpack(
            pl.ds(pl.multiple_of(RIM + i * step_rows, 8), step_rows),
            pl.ds(pl.multiple_of(TOP + i * step_rows, 8), step_rows),
            step_rows,
            has_right,
            has_left,
        )

    for source, ok in ((0, has_up), (RIM + TILE, has_down)):
        unpack(
            pl.ds(source, RIM),
            pl.ds(TOP - RIM + source, RIM),
            RIM,
            jnp.logical_and(has_right, ok),
            jnp.logical_and(has_left, ok),
        )

    balance(0, 2)

    @pl.loop(0, TILE // FAC // 4)
    def _(i):
        for k in range(4):
            balance(4 * i + 1 + k, 2)

    def sweep(now, later):
        for q in range((TILE + 2 * RIM) // 16):
            base = TOP - RIM + 16 * q
            rows = pl.ds(base, 16)
            lane = iota((16, 128), 1)
            sums = {-1: [], 0: [], 1: []}
            middle = []
            for t in range(3):
                parts = {-1: None, 0: None, 1: None}
                for down_row in (-1, 0, 1):
                    at = pl.ds(base - down_row, 16)
                    out = now[t, at, :]
                    if down_row == 0:
                        middle.append(out)
                    for direction, (dr, dc) in enumerate(OFFSETS):
                        if dr == down_row:
                            term = ext[WEIGHT + direction, t, at, :] * out
                            parts[dc] = term if parts[dc] is None else parts[dc] + term
                for dc in (-1, 0, 1):
                    sums[dc].append(parts[dc])
            east = [pltpu.roll(x, 1, 1) for x in sums[1]]
            west = [pltpu.roll(x, 127, 1) for x in sums[-1]]
            for t in range(3):
                inflow = (
                    sums[0][t]
                    + jnp.where(lane == 0, east[(t + 2) % 3], east[t])
                    + jnp.where(lane == 127, west[(t + 1) % 3], west[t])
                )
                storage = (ext[STORE, t, rows, :] - middle[t]) + inflow
                ext[STORE, t, rows, :] = storage
                later[t, rows, :] = ext[RATE, t, rows, :] * storage
                if t < 2:
                    drained[t, rows, :] = drained[t, rows, :] + middle[t]

    @pl.loop(0, SWEEPS // 2)
    def _(i):
        @pl.when(i == 1)
        def _():
            @pl.loop(1, SIDE)
            def _(k):
                slot = lax.rem(across + k, SIDE)
                matrix_copy(slot, slot).wait_recv()

            after[1] = mats[SIDE - 1]
            tmat[1] = mats[jnp.where(across > 0, across - 1, SIDE)]

        after[i + 1] = product(after[i], mats[jnp.where(i > 0, SIDE - 1 - i, SIDE)])
        started = jnp.logical_and(i > 0, i < across)
        tmat[i + 1] = product(tmat[i], mats[jnp.where(started, across - 1 - i, SIDE)])
        sweep(first_out, second_out)
        sweep(second_out, first_out)

    def group_copy(to, slot):
        return pltpu.make_async_remote_copy(
            src_ref=after.at[SIDE],
            dst_ref=gmats.at[slot],
            send_sem=qsend.at[to],
            recv_sem=qrecv.at[slot],
            device_id=(r, to * SIDE + across),
            device_id_type=MESH,
        )

    @pl.loop(group + 1, n_col // SIDE)
    def _(later):
        group_copy(later, group).start()

    for t in range(2):
        own = pl.ds(TOP, TILE)
        ground_out[t, own, :] = ext[STORE, t, own, :]
        drained[t, own, :] = drained[t, own, :] * retained[t, own, :]

    def build(piece):
        top = iota((8, 128), 0)
        for b in range(NBLK):
            for i in range(4 * piece, 4 * piece + 4):
                for t in range(2):
                    lanes = pl.ds(TILE * i + 128 * t, 128)
                    row = b * BR + i
                    same = lax.shift_right_logical(seg[t, row : row + 1, :], 4) == top
                    kept = jnp.where(same, drained[t, TOP + row : TOP + row + 1, :], 0.0)
                    high, low = split(kept)
                    ahot[16 * b : 16 * b + 8, lanes] = high
                    ahot[16 * b + 8 : 16 * b + 16, lanes] = low

    build(0)
    for i in range(4):
        if i < 3:
            build(i + 1)
        wide = pl.ds(4 * TILE * i, 4 * TILE)
        piece = nt(ahot[:, wide], bhot[:, wide])
        for t in range(2):
            half = piece[:, 128 * t : 128 * t + 128]
            hot[t] = half if i == 0 else hot[t] + half

    lane = iota((8, 128), 1)
    sixteen = lax.shift_right_logical(lane, 4)
    for b in range(NBLK):
        t = b // 8
        x = hot[t, b * 16 : b * 16 + 8, :] + hot[t, b * 16 + 8 : b * 16 + 16, :]
        x = jnp.where(sixteen == b % 8, x, 0.0)
        for shift in (16, 32, 64):
            x = x + pltpu.roll(x, shift, 1)
        x = jnp.where(sixteen == iota((8, 128), 0), x, 0.0)
        lat[b : b + 1, :] = 0.001 * jnp.sum(x, axis=0, keepdims=True)

    def to_row(matrix):
        column = jnp.sum(matrix, axis=1, keepdims=True)
        same = iota((SEG, SEG), 0) == iota((SEG, SEG), 1)
        return jnp.sum(jnp.where(same, column, 0.0), axis=0, keepdims=True)

    total = wmat[0] * lat[0:1, :]
    for b in range(1, NBLK):
        total = total + wmat[b] * lat[b : b + 1, :]
    leaving = to_row(total)
    gsend[0:1, :] = leaving
    gsend[1:2, :] = to_row(after[SIDE - 1 - across] * leaving)

    def leaving_copy(col, slot):
        return pltpu.make_async_remote_copy(
            src_ref=gsend,
            dst_ref=gin.at[slot],
            send_sem=gsend_sem.at[col],
            recv_sem=grecv.at[slot],
            device_id=(r, col),
            device_id_type=MESH,
        )

    @pl.loop(c + 1, n_col)
    def _(col):
        leaving_copy(col, c).start()

    @pl.loop(0, NBLK)
    def _(b):
        source = lat[pl.ds(b, 1), :]
        carried = jnp.zeros((SEG, SEG), F32)
        for back in range(1, 4):
            share = trans[pl.ds(b + 3 - back, 1), :] * drains_here(b, back)
            carried = carried + fmat[b + 3 - back] * share
            source = source + share * flow0[pl.ds(b + 3 - back, 1), :]
        fmat[b + 3] = product_nt(carried, inv[b])
        flow0[pl.ds(b + 3, 1), :] = to_row(inv[b] * source)

    @pl.loop(0, group)
    def _(slot):
        group_copy(group, slot).wait_recv()

    reach = [tmat[across]]
    for j in range(n_col // SIDE - 2):
        slot = jnp.where(j < group, group - 1 - j, n_col // SIDE)
        reach.append(product(reach[j], gmats[slot]))

    @pl.loop(0, c)
    def _(slot):
        leaving_copy(c, slot).wait_recv()

    total = jnp.zeros((SEG, SEG), F32)
    for j in range(n_col // SIDE - 1):
        arriving = jnp.zeros((1, SEG), F32)
        for k in range(SIDE):
            slot = jnp.where(j < group, (group - 1 - j) * SIDE + k, c)
            arriving = arriving + gin[slot, 1:2, :]
        total = total + reach[j] * arriving
    for k in range(SIDE - 1):
        slot = jnp.where(k < across, c - 1 - k, c)
        total = total + tmat[k] * gin[slot, 0:1, :]
    entering = jnp.sum(total, axis=1, keepdims=True)

    for b in range(NBLK):
        extra = jnp.sum(fmat[b + 3] * entering, axis=0, keepdims=True)
        flow_out[b : b + 1, :] = flow0[b + 3 : b + 4, :] + extra

    for half, needed in ((0, low_half), (1, high_half)):

        @pl.when(needed)
        def _():
            many(n_col // 2, 0, half).wait_send()

        @pl.when(jnp.logical_not(needed))
        def _():
            many(n_col // 2 + 1, 0, half).wait_send()

        for sem, sends in ((1, sends_down), (2, sends_up)):

            @pl.when(sends)
            def _():
                many(n_col // 2 + 1, sem, half).wait_send()

    @pl.loop(1, SIDE)
    def _(k):
        matrix_copy(lax.rem(across + k, SIDE), across).wait_send()

    @pl.loop(group + 1, n_col // SIDE)
    def _(later):
        group_copy(later, group).wait_send()

    each_strip(lambda copy: copy.wait_send(), True)

    @pl.loop(c + 1, n_col)
    def _(col):
        leaving_copy(col, c).wait_send()


def writer(*refs):
    snow, soil, water, flow, snow_out, soil_out, ground_out, flow_out, sems = refs
    copies = [pltpu.make_async_copy(flow, flow_out, sems.at[6])]
    for k, (ref, out) in enumerate(((snow, snow_out), (soil, soil_out), (water, ground_out))):
        for t in range(2):
            copies.append(
                pltpu.make_async_copy(
                    ref.at[t, pl.ds(TOP, TILE), :],
                    out.at[:, pl.ds(128 * t, 128)],
                    sems.at[2 * k + t],
                )
            )
    for copy in copies:
        copy.start()
    for copy in copies:
        copy.wait()


def per_device(n_row, n_col, forcing, *args):
    *args, downstream = args
    cells = forcing.shape[2]
    any_space = pl.BlockSpec(memory_space=pl.ANY)
    vmem = pl.BlockSpec(memory_space=pltpu.VMEM)
    smem = pl.BlockSpec(memory_space=pltpu.SMEM)
    tile = jax.ShapeDtypeStruct((TILE, TILE), F32)
    flows = jax.ShapeDtypeStruct((NBLK, SEG), F32)
    dma = pltpu.SemaphoreType.DMA
    results = pl.pallas_call(
        functools.partial(kernel, n_row, n_col),
        out_shape=(*(pltpu.VMEM((2, ROWS, 128), F32) for _ in range(3)), pltpu.VMEM((NBLK, SEG), F32)),
        in_specs=[vmem] + [any_space] * 9 + [vmem, smem],
        out_specs=(vmem, vmem, vmem, vmem),
        scratch_shapes=[
            pltpu.VMEM((ARRAYS, 3, ROWS, 128), F32),
            pltpu.VMEM((8, TILE, TILE), BF16),
            pltpu.VMEM((2, TILE, 128), jnp.int32),
            pltpu.VMEM((NBLK, SEG, SEG), F32),
            pltpu.VMEM((NBLK + 1, SEG, SEG), F32),
            pltpu.VMEM((NBLK + 3, SEG, SEG), F32),
            pltpu.VMEM((SIDE + 1, SEG, SEG), F32),
            pltpu.VMEM((SIDE + 1, SEG, SEG), F32),
            pltpu.VMEM((SIDE + 1, SEG, SEG), F32),
            pltpu.VMEM((n_col // SIDE + 1, SEG, SEG), F32),
            pltpu.VMEM((TILE, BR * TILE), BF16),
            pltpu.VMEM((TILE, BR * TILE), BF16),
            pltpu.VMEM((2, TILE, 128), F32),
            pltpu.VMEM((2, TILE, 128), F32),
            pltpu.VMEM((2, TILE + 2 * RIM, 128), F32),
            pltpu.VMEM((2, 8, RIM, TILE), BF16),
            pltpu.VMEM((2, 8, cells // 2), F32),
            pltpu.VMEM((2, n_col + 2, 8, cells // 2), F32),
            pltpu.VMEM((cells, 384), BF16),
            pltpu.VMEM((2, 3, (n_col + 2) * 8, 128), F32),
            pltpu.VMEM((3, ROWS, 128), F32),
            pltpu.VMEM((3, ROWS, 128), F32),
            pltpu.VMEM((2, ROWS, 128), F32),
            pltpu.VMEM((2, ROWS, 128), F32),
            pltpu.VMEM((24, SEG), F32),
            pltpu.VMEM((NBLK, SEG), F32),
            pltpu.VMEM((24, SEG), F32),
            pltpu.VMEM((8, SEG), F32),
            pltpu.VMEM((n_col, 8, SEG), F32),
            dma((4,)),
            dma((6,)),
            dma((6,)),
            dma((6,)),
            dma((6,)),
            dma((4,)),
            dma((4,)),
            dma((SIDE,)),
            dma((SIDE,)),
            dma((n_col // SIDE,)),
            dma((n_col // SIDE,)),
            dma((n_col,)),
            dma((n_col,)),
        ],
        compiler_params=pltpu.CompilerParams(
            collective_id=0, has_side_effects=True
        ),
        name="hydrology",
    )(forcing, *args, downstream.T)
    return pl.pallas_call(
        writer,
        out_shape=(tile, tile, tile, flows),
        in_specs=[any_space] * 4,
        out_specs=(any_space,) * 4,
        scratch_shapes=[dma((7,))],
        compiler_params=pltpu.CompilerParams(vmem_limit_bytes=1 << 20),
        name="writer",
    )(*results)


def solution(mesh):
    n_row, n_col = mesh.shape["row"], mesh.shape["col"]
    tiles = P("row", "col")
    placed = (
        P(None, ("row", "col"), None),
        *(tiles for _ in range(6)),
        P(None, "row", "col"),
        tiles,
        P("row", "col", None),
        tiles,
        tiles,
    )
    return jax.shard_map(
        functools.partial(per_device, n_row, n_col),
        mesh=mesh,
        in_specs=placed,
        out_specs=(tiles, tiles, tiles, tiles),
        check_vma=False,
    )
```
